32 devices in a mesh: gy: 4 (over y, core), gx: 8 (over z, x).
Axes of the slice: x: 2, y: 2, z: 4, core: 2. Of those that a mesh axis runs over, the one named last changes fastest.
Arguments:
- phase: float32 [2, 128, 1024], P(None, 'gy', 'gx'), may hold values from -1.5 to 1.5
- velocity: float32 [2, 128, 1024], P(None, 'gy', 'gx'), may hold values from -2 to 2
- offsets: int32 [2, 4], replicated, may hold values from 0 to 1020, as said below
Outputs:
- phase_out: float32 [2, 128, 1024], P(None, 'gy', 'gx')
The draws below stay inside these ranges and needn't reach their ends.
Inputs may be any that keep to these rules, and one draw needn't show every extreme that they name: `offsets`: every offset is a multiple of 2 ** 2.
All inputs are finite; a program needn't handle non-finite values.
Results may differ from the reference program's by a relative error of at most 0.00014.
Values sent between devices are 32-bit elements; how exact they have to be, the bound alone decides.
No kernel may reach another device: no remote copies, remote signals or barrier semaphores. Data moves between devices by JAX's collectives and lax.ppermute only.
A program may use at most 64 MiB of HBM per device.

```python
import jax
import jax.numpy as jnp

CY = 32
NZ = 2
STEPS = 2
ITERS = 2
LEVELS = 3
COARSE = 4
NX = 1024
NY = 128
N_GY = 4


def draw_offsets(key, part):
    spacing = 2 ** (LEVELS - 1)
    return jax.random.randint(key, (STEPS, N_GY), 0, NX // spacing, dtype=jnp.int32) * spacing


def levels(own_key, shape, shards, least, top_value):
    loudness, own = 1.0, jax.random.fold_in(own_key, 6)
    for position, parts in shards:
        heights = jnp.exp(jax.random.uniform(jax.random.fold_in(own, position), (parts,), jnp.float32, least / len(shards), top_value / len(shards)))
        loudness = loudness * jnp.repeat(heights, shape[position] // parts).reshape([-1 if axis == position else 1 for axis in range(len(shape))])
    return loudness


def setup_inputs(seed: int = 0) -> dict:
    splits = jax.random.split(jax.random.key(seed), 4)
    return {
        "phase": jnp.clip(jax.random.uniform(splits[0], (NZ, NY, NX), jnp.float32, -1.5, 1.5) * levels(splits[0], (NZ, NY, NX), ((1, 4), (2, 8)), -0.4, 0.0), -1.5, 1.5),
        "velocity": jnp.clip(jax.random.uniform(splits[1], (NZ, NY, NX), jnp.float32, -2.0, 2.0) * levels(splits[1], (NZ, NY, NX), ((1, 4), (2, 8)), -0.4, 0.0), -2.0, 2.0),
        "offsets": draw_offsets(jax.random.fold_in(splits[3], 71), 0),
    }


RELAXATION = 0.8
DIFFUSION = 4.0
VERTICAL = 1.0
REACTION = 0.5
ADVECTION = 0.5


def neighbours(field, offsets_now, block_rows):
    planes, height, breadth = field.shape
    blocks = field.reshape(planes, N_GY, block_rows, breadth)
    columns = jnp.arange(breadth, dtype=jnp.int32)
    first_rows = blocks[:, :, 0, :]
    last_rows = blocks[:, :, -1, :]
    next_first = jnp.roll(first_rows, -1, axis=1)
    next_offsets = jnp.roll(offsets_now, -1)
    upper_index = (columns[None, :] + next_offsets[:, None]) % breadth
    above_rows = jnp.take_along_axis(next_first, jnp.broadcast_to(upper_index[None], next_first.shape), axis=2)
    previous_last = jnp.roll(last_rows, 1, axis=1)
    lower_index = (columns[None, :] - offsets_now[:, None]) % breadth
    below_rows = jnp.take_along_axis(previous_last, jnp.broadcast_to(lower_index[None], previous_last.shape), axis=2)
    upward = jnp.concatenate([blocks[:, :, 1:, :], above_rows[:, :, None, :]], axis=2).reshape(planes, height, breadth)
    downward = jnp.concatenate([below_rows[:, :, None, :], blocks[:, :, :-1, :]], axis=2).reshape(planes, height, breadth)
    return upward + downward + jnp.roll(field, 1, 2) + jnp.roll(field, -1, 2)


def operate(field, offsets_now, block_rows, coupling):
    diagonal = 1.0 + 4.0 * coupling + 2.0 * VERTICAL
    vertical_sum = jnp.roll(field, 1, 0) + jnp.roll(field, -1, 0)
    return diagonal * field - coupling * neighbours(field, offsets_now, block_rows) - VERTICAL * vertical_sum


def vcycle(residual, offsets_raw, layer_index):
    factor = 2 ** layer_index
    coupling = DIFFUSION / 4.0 ** layer_index
    diagonal = 1.0 + 4.0 * coupling + 2.0 * VERTICAL
    offsets_now = (offsets_raw // factor).astype(jnp.int32)
    block_rows = CY // factor
    estimate = RELAXATION * residual / diagonal
    if layer_index == LEVELS - 1:
        for sweep_index in range(COARSE - 1):
            estimate = estimate + RELAXATION * (residual - operate(estimate, offsets_now, block_rows, coupling)) / diagonal
        return estimate
    defect = residual - operate(estimate, offsets_now, block_rows, coupling)
    planes, height, breadth = defect.shape
    coarser = defect.reshape(planes, height // 2, 2, breadth // 2, 2).mean(axis=(2, 4))
    correction = vcycle(coarser, offsets_raw, layer_index + 1)
    estimate = estimate + jnp.repeat(jnp.repeat(correction, 2, axis=1), 2, axis=2)
    estimate = estimate + RELAXATION * (residual - operate(estimate, offsets_now, block_rows, coupling)) / diagonal
    return estimate


def reference(phase, velocity, offsets):
    phase_now = phase
    for time_step in range(STEPS):
        offsets_raw = offsets[time_step]
        source = phase_now + REACTION * (phase_now - phase_now * phase_now * phase_now) - ADVECTION * velocity * (jnp.roll(phase_now, -1, 2) - jnp.roll(phase_now, 1, 2))
        residual = source - operate(phase_now, offsets_raw, CY, DIFFUSION)
        precond = vcycle(residual, offsets_raw, 0)
        projected = jnp.sum(residual * precond)
        direction = precond
        for iteration in range(ITERS):
            image = operate(direction, offsets_raw, CY, DIFFUSION)
            step_size = projected / jnp.sum(direction * image)
            phase_now = phase_now + step_size * direction
            residual = residual - step_size * image
            if iteration + 1 < ITERS:
                precond = vcycle(residual, offsets_raw, 0)
                following = jnp.sum(residual * precond)
                direction = precond + (following / projected) * direction
                projected = following
    return phase_now
```

```python
import jax
import jax.numpy as jnp
from jax import lax
from jax.experimental import pallas as pl
from jax.experimental.pallas import tpu as pltpu
from jax.sharding import PartitionSpec as P

STEPS = 2
ITERS = 2
LEVELS = 3
COARSE = 4

RELAXATION = 0.8
DIFFUSION = 4.0
VERTICAL = 1.0
REACTION = 0.5
ADVECTION = 0.5

LANES = 128
SUB = 8


class Level:
    def __init__(self, index, pages, strip_rows, strips, planes):
        self.pages = pages >> index
        self.rows = strip_rows >> index
        self.strips = strips
        self.planes = planes
        self.pitch = self.rows + SUB
        self.height = strips * self.pitch + SUB
        self.factor = 2**index
        self.coupling = DIFFUSION / 4.0**index
        self.diagonal = 1.0 + 4.0 * self.coupling + 2.0 * VERTICAL
        self.relax = RELAXATION / self.diagonal
        self.tiles = self.rows // SUB
        self.count = self.pages * planes

    def shape(self):
        return (self.count * self.height, LANES)

    def base(self, strip, tile):
        return pl.multiple_of(SUB + strip * self.pitch + tile * SUB, SUB)


def tile_of(ref, level, page, plane, row):
    return ref[pl.ds((page * level.planes + plane) * level.height + row, SUB), :]


def put_tile(ref, level, page, plane, row, value):
    ref[pl.ds((page * level.planes + plane) * level.height + row, SUB), :] = value


def fill_halo(ref, level, offsets, step, halo):
    count, width = level.count, level.pages
    for strip in range(level.strips):
        shift = offsets[step, strip] // level.factor
        lane, page = shift // width, shift % width
        under = (strip - 1) % level.strips
        first = SUB + strip * level.pitch
        last = SUB + under * level.pitch + level.rows - 1
        upper = ref[pl.ds(first, count, stride=level.height), :]
        lower = ref[pl.ds(last, count, stride=level.height), :]
        start = strip * 4 * count
        halo[pl.ds(start, count), :] = pltpu.roll(upper, (LANES - lane) % LANES, 1)
        halo[pl.ds(start + count, count), :] = pltpu.roll(upper, LANES - 1 - lane, 1)
        halo[pl.ds(start + 2 * count, count), :] = pltpu.roll(lower, (lane + 1) % LANES, 1)
        halo[pl.ds(start + 3 * count, count), :] = pltpu.roll(lower, lane, 1)
        ref[pl.ds(last + 1, count, stride=level.height), :] = halo[pl.ds(start + page * level.planes, count), :]
        ref[pl.ds(first - 1, count, stride=level.height), :] = halo[
            pl.ds(start + 2 * count + (width - page) * level.planes, count), :
        ]


def stencil(ref, level, base):
    planes, width = level.planes, level.pages
    cell = [[tile_of(ref, level, p, z, base) for z in range(planes)] for p in range(width)]
    out = []
    for p in range(width):
        row = []
        for z in range(planes):
            right = cell[p + 1][z] if p + 1 < width else pltpu.roll(cell[0][z], LANES - 1, 1)
            left = cell[p - 1][z] if p else pltpu.roll(cell[width - 1][z], 1, 1)
            above = tile_of(ref, level, p, z, base + 1)
            below = tile_of(ref, level, p, z, base - 1)
            beside = (above + below) + (right + left)
            vertical = cell[p][(z + 1) % planes] + cell[p][(z - 1) % planes]
            row.append((cell[p][z], right, left, beside, vertical))
        out.append(row)
    return out


def smooth(level, cell, beside, vertical):
    k = level.relax
    return (1.0 - k * level.diagonal) * cell + (k * level.coupling) * beside + (k * VERTICAL) * vertical


def apply(level, cell, beside, vertical):
    return level.diagonal * cell - level.coupling * beside - VERTICAL * vertical


def restrict(ref, level, coarse_ref, coarse, pairs):
    planes = level.planes

    def body(index, carry):
        strip, tile = index // coarse.tiles, index % coarse.tiles
        for half in range(2):
            base = level.base(strip, 2 * tile + half)
            terms = stencil(ref, level, base)
            for p in range(coarse.pages):
                for z in range(planes):
                    total = 0.0
                    for q in (2 * p, 2 * p + 1):
                        cell, _, _, beside, vertical = terms[q][z]
                        total = total + smooth(level, cell, beside, vertical)
                    pairs[pl.ds((p * planes + z) * 2 * SUB + half * SUB, SUB), :] = total
        for p in range(coarse.pages):
            for z in range(planes):
                start = (p * planes + z) * 2 * SUB
                even = pairs[pl.ds(start, SUB, stride=2), :]
                odd = pairs[pl.ds(start + 1, SUB, stride=2), :]
                put_tile(coarse_ref, coarse, p, z, coarse.base(strip, tile), 0.25 * (even + odd))
        return carry

    lax.fori_loop(0, coarse.strips * coarse.tiles, body, 0)


def prolong(coarse_ref, coarse, residual, level, ref, pairs):
    planes = level.planes

    def body(index, carry):
        strip, tile = index // coarse.tiles, index % coarse.tiles
        for p in range(coarse.pages):
            for z in range(planes):
                start = (p * planes + z) * 2 * SUB
                value = tile_of(coarse_ref, coarse, p, z, coarse.base(strip, tile))
                pairs[pl.ds(start, SUB, stride=2), :] = value
                pairs[pl.ds(start + 1, SUB, stride=2), :] = value
        for p in range(coarse.pages):
            for z in range(planes):
                start = (p * planes + z) * 2 * SUB
                for half in range(2):
                    value = pairs[pl.ds(start + half * SUB, SUB), :]
                    base = level.base(strip, 2 * tile + half)
                    for q in (2 * p, 2 * p + 1):
                        put_tile(ref, level, q, z, base, level.relax * tile_of(residual, level, q, z, base) + value)
        return carry

    lax.fori_loop(0, coarse.strips * coarse.tiles, body, 0)


def per_tile(level, body, sums):
    def step(index, carry):
        return body(level.base(index // level.tiles, index % level.tiles), carry)

    zero = jnp.zeros((SUB, LANES), jnp.float32)
    return lax.fori_loop(0, level.strips * level.tiles, step, (zero,) * sums)


def total(vector):
    return jnp.sum(jnp.sum(vector, axis=0, keepdims=True), axis=1, keepdims=True)


def relaxed(ref, residual, level, target):
    def body(base, carry):
        for p, row in enumerate(stencil(ref, level, base)):
            for z, (cell, _, _, beside, vertical) in enumerate(row):
                value = smooth(level, cell, beside, vertical) + level.relax * tile_of(residual, level, p, z, base)
                put_tile(target, level, p, z, base, value)
        return carry

    per_tile(level, body, 0)


def coarsest(residual, level, offsets, step, spare, halo):
    def first(base, carry):
        for p, row in enumerate(stencil(residual, level, base)):
            for z, (cell, _, _, beside, vertical) in enumerate(row):
                put_tile(spare[0], level, p, z, base, level.relax * (cell + smooth(level, cell, beside, vertical)))
        return carry

    fill_halo(residual, level, offsets, step, halo)
    per_tile(level, first, 0)
    now = 0
    for _ in range(COARSE - 2):
        fill_halo(spare[now], level, offsets, step, halo)
        relaxed(spare[now], residual, level, spare[1 - now])
        now = 1 - now
    return spare[now]


def vcycle(residual, levels, index, offsets, step, work, halo, pairs):
    level, coarse = levels[index], levels[index + 1]
    below, estimate = work[index + 1], work[index][1]
    fill_halo(residual, level, offsets, step, halo)
    restrict(residual, level, below[0], coarse, pairs)
    if index + 2 == LEVELS:
        correction = coarsest(below[0], coarse, offsets, step, below[1:], halo)
    else:
        vcycle(below[0], levels, index + 1, offsets, step, work, halo, pairs)
        correction = below[2]
        relaxed(below[1], below[0], coarse, correction)
    prolong(correction, coarse, residual, level, estimate, pairs)
    fill_halo(estimate, level, offsets, step, halo)


def interleave(ref, level):
    width, planes = level.pages, level.planes
    lane = lax.broadcasted_iota(jnp.int32, (SUB, LANES), 1)
    per = LANES // width
    source = (lane % per) * width + lane // per

    def body(index, carry):
        base = level.base(index // level.tiles, index % level.tiles)
        for z in range(planes):
            pages = [tile_of(ref, level, p, z, base) for p in range(width)]
            bit = 1
            while bit < width:
                low = (lane // bit) % 2 == 0
                for p in range(width):
                    if not p & bit:
                        a, b = pages[p], pages[p | bit]
                        pages[p] = jnp.where(low, a, pltpu.roll(b, bit, 1))
                        pages[p | bit] = jnp.where(low, pltpu.roll(a, LANES - bit, 1), b)
                bit *= 2
            for p in range(width):
                put_tile(ref, level, p, z, base, jnp.take_along_axis(pages[p], source, axis=1))
        return carry

    lax.fori_loop(0, level.strips * level.tiles, body, 0)


def solve(offsets, u, v, r, q, w, work, halo, pairs, levels):
    fine = levels[0]
    e = work[0][1]
    update = None
    for step in range(STEPS):
        fill_halo(u, fine, offsets, step, halo)

        def residual(base, carry):
            for p, row in enumerate(stencil(u, fine, base)):
                for z, (cell, right, left, beside, vertical) in enumerate(row):
                    speed = tile_of(v, fine, p, z, base)
                    cube = cell * cell * cell
                    value = (
                        (1.0 + REACTION - fine.diagonal) * cell
                        - REACTION * cube
                        - ADVECTION * speed * (right - left)
                        + fine.coupling * beside
                        + VERTICAL * vertical
                    )
                    put_tile(r, fine, p, z, base, value)
            return carry

        per_tile(fine, residual, 0)
        vcycle(r, levels, 0, offsets, step, work, halo, pairs)

        def finish(base, carry):
            (rw,) = carry
            for p, row in enumerate(stencil(e, fine, base)):
                for z, (cell, _, _, beside, vertical) in enumerate(row):
                    res = tile_of(r, fine, p, z, base)
                    value = smooth(fine, cell, beside, vertical) + fine.relax * res
                    put_tile(w, fine, p, z, base, value)
                    rw = rw + res * value
            return (rw,)

        (rw,) = per_tile(fine, finish, 1)
        rw = total(rw)
        fill_halo(w, fine, offsets, step, halo)

        def image(base, carry):
            (wq,) = carry
            for p, row in enumerate(stencil(w, fine, base)):
                for z, (cell, _, _, beside, vertical) in enumerate(row):
                    value = apply(fine, cell, beside, vertical)
                    put_tile(q, fine, p, z, base, value)
                    wq = wq + cell * value
            return (wq,)

        (wq,) = per_tile(fine, image, 1)
        alpha = rw / total(wq)
        vcycle(q, levels, 0, offsets, step, work, halo, pairs)

        def finish_next(base, carry):
            (rw,) = carry
            for p, row in enumerate(stencil(e, fine, base)):
                for z, (cell, _, _, beside, vertical) in enumerate(row):
                    img = tile_of(q, fine, p, z, base)
                    value = smooth(fine, cell, beside, vertical) + fine.relax * img
                    res = tile_of(r, fine, p, z, base) - alpha * img
                    value = tile_of(w, fine, p, z, base) - alpha * value
                    put_tile(r, fine, p, z, base, value)
                    rw = rw + res * value
            return (rw,)

        (following,) = per_tile(fine, finish_next, 1)
        following = total(following)
        beta = following / rw
        fill_halo(r, fine, offsets, step, halo)

        def image_next(base, carry):
            (pq,) = carry
            for p, row in enumerate(stencil(r, fine, base)):
                for z, (cell, _, _, beside, vertical) in enumerate(row):
                    direction = cell + beta * tile_of(w, fine, p, z, base)
                    value = apply(fine, cell, beside, vertical) + beta * tile_of(q, fine, p, z, base)
                    pq = pq + direction * value
            return (pq,)

        (pq,) = per_tile(fine, image_next, 1)
        alpha_next = following / total(pq)
        along = alpha + alpha_next * beta

        def update(base, carry):
            for p in range(fine.pages):
                for z in range(fine.planes):
                    value = (
                        tile_of(u, fine, p, z, base)
                        + along * tile_of(w, fine, p, z, base)
                        + alpha_next * tile_of(r, fine, p, z, base)
                    )
                    put_tile(u, fine, p, z, base, value)
            return carry

        if step + 1 < STEPS:
            per_tile(fine, update, 0)
    return update


def whole_kernel(keys, levels, *refs):
    count = len(keys)
    offsets, blocks, out = refs[0], refs[1 : 1 + count], refs[1 + count]
    u, v, r, q, w, e, r1, e1, f1, r2, e2, f2, halo, pairs, sems = refs[2 + count :]
    fine = levels[0]
    gy, gx = lax.axis_index("gy"), lax.axis_index("gx")
    copies = []
    for index, (name, dy, dx) in enumerate(keys):
        target = u if name == "u" else v
        row = SUB + jnp.bitwise_xor(gy, dy) * fine.pitch
        for z in range(fine.planes):
            start = (jnp.bitwise_xor(gx, dx) * fine.planes + z) * fine.height + row
            copy = pltpu.make_async_copy(
                blocks[index].at[z],
                target.at[pl.ds(pl.multiple_of(start, SUB), fine.rows), :],
                sems.at[index * fine.planes + z],
            )
            copy.start()
            copies.append(copy)
    for copy in copies:
        copy.wait()
    interleave(u, fine)
    interleave(v, fine)
    work = [[r, e], [r1, e1, f1], [r2, e2, f2]]
    update = solve(offsets, u, v, r, q, w, work, halo, pairs, levels)
    lane = lax.broadcasted_iota(jnp.int32, (SUB, LANES), 1)
    source = gx * (LANES // fine.pages) + lane // fine.pages
    for tile in range(fine.tiles):
        base = fine.base(gy, tile)
        update(base, ())
        for z in range(fine.planes):
            value = jnp.zeros((SUB, LANES), jnp.float32)
            for p in range(fine.pages):
                page = jnp.take_along_axis(tile_of(u, fine, p, z, base), source, axis=1)
                value = jnp.where(lane % fine.pages == p, page, value)
            out[z, pl.ds(tile * SUB, SUB), :] = value


def on_whole(blocks, offsets, strips, width):
    keys = sorted(blocks)
    planes, rows, columns = blocks[keys[0]].shape
    levels = [Level(i, width, rows, strips, planes) for i in range(LEVELS)]
    fields = [pltpu.VMEM(levels[0].shape(), jnp.float32)] * 6
    fields += [pltpu.VMEM(levels[1].shape(), jnp.float32)] * 3 + [pltpu.VMEM(levels[2].shape(), jnp.float32)] * 3
    count = levels[0].count
    scratch = fields + [
        pltpu.VMEM((strips * 4 * count, LANES), jnp.float32),
        pltpu.VMEM((count * SUB, LANES), jnp.float32),
        pltpu.SemaphoreType.DMA((len(keys) * planes,)),
    ]

    def kernel(*refs):
        whole_kernel(keys, levels, *refs)

    return pl.pallas_call(
        kernel,
        out_shape=jax.ShapeDtypeStruct((planes, rows, columns), jnp.float32),
        in_specs=[pl.BlockSpec(memory_space=pltpu.SMEM)] + [pl.BlockSpec(memory_space=pl.ANY)] * len(keys),
        out_specs=pl.BlockSpec(memory_space=pltpu.VMEM),
        scratch_shapes=scratch,
        compiler_params=pltpu.CompilerParams(vmem_limit_bytes=48 << 20),
    )(offsets, *[blocks[key] for key in keys])


def swapped(block, axis, bits):
    count = lax.axis_size(axis)
    return lax.ppermute(block, axis, [(i, i ^ bits) for i in range(count)])


def gathered(phase, velocity):
    out = {}
    for name, own in (("u", phase), ("v", velocity)):
        out[name, 0, 0] = own
        for k in (2, 4, 6):
            out[name, 0, k] = swapped(own, "gx", k)
        for k in (0, 2, 4, 6):
            out[name, 0, k | 1] = swapped(out[name, 0, k], "gx", 1)
            out[name, 2, k] = swapped(out[name, 0, k], "gy", 2)
            out[name, 2, k | 1] = swapped(out[name, 2, k], "gx", 1)
    for (name, dy, dx), block in list(out.items()):
        out[name, dy ^ 1, dx] = swapped(block, "gy", 1)
    return out


def padded(cells, sides, width):
    for axis, dim in sides:
        count = lax.axis_size(axis)
        head = lax.slice_in_dim(cells, 0, width, axis=dim)
        tail = lax.slice_in_dim(cells, cells.shape[dim] - width, cells.shape[dim], axis=dim)
        cells = jnp.concatenate(
            [
                lax.ppermute(tail, axis, [(i, (i + 1) % count) for i in range(count)]),
                cells,
                lax.ppermute(head, axis, [((i + 1) % count, i) for i in range(count)]),
            ],
            axis=dim,
        )
    return cells


def sheared(bottom_row, upper_row, offsets_now, anchor, columns):
    breadth = bottom_row.shape[1]
    device_row = lax.axis_index("gy")
    row_count = lax.axis_size("gy")
    below_shift = offsets_now[device_row]
    above_shift = offsets_now[(device_row + 1) % row_count]
    local_columns = jnp.arange(columns, dtype=jnp.int32)
    down_index = (anchor + below_shift + local_columns) % breadth
    up_index = (anchor - above_shift + local_columns) % breadth
    down_window = jnp.take(bottom_row, down_index, axis=1)
    up_window = jnp.take(upper_row, up_index, axis=1)
    stacked = jnp.stack([down_window, up_window], axis=1)
    rims = padded(stacked, (("gy", 1),), 1)
    return (rims[:, 0, :], rims[:, 3, :])


def block_stencil(field, below_row, above_row, across, coupling):
    diagonal = 1.0 + 4.0 * coupling + 2.0 * VERTICAL
    column_pad = jnp.concatenate([below_row[:, None, :], field, above_row[:, None, :]], axis=1)
    beside = column_pad[:, 2:, :] + column_pad[:, :-2, :] + across
    vertical_sum = jnp.roll(field, 1, 0) + jnp.roll(field, -1, 0)
    return diagonal * field - coupling * beside - VERTICAL * vertical_sum


def block_operate(field, offsets_now, coupling):
    columns = field.shape[2]
    margins = padded(field, (("gx", 2),), 1)
    bottom_full, upper_full = (
        lax.all_gather(field[:, 0, :], "gx", axis=1, tiled=True),
        lax.all_gather(field[:, -1, :], "gx", axis=1, tiled=True),
    )
    right_field = margins[:, :, 2:]
    left_field = margins[:, :, :-2]
    below_row, above_row = sheared(
        bottom_full, upper_full, offsets_now, lax.axis_index("gx") * columns, columns
    )
    across = right_field + left_field
    return (block_stencil(field, below_row, above_row, across, coupling), right_field, left_field)


def block_operate_strip(field, offsets_now, coupling):
    below_row, above_row = sheared(field[:, 0, :], field[:, -1, :], offsets_now, 0, field.shape[2])
    across = jnp.roll(field, 1, 2) + jnp.roll(field, -1, 2)
    return block_stencil(field, below_row, above_row, across, coupling)


def block_coarsest(residual, offsets_now, coupling):
    diagonal = 1.0 + 4.0 * coupling + 2.0 * VERTICAL
    columns = residual.shape[2]
    gathered = lax.all_gather(residual, "gx", axis=2, tiled=True)
    estimate = RELAXATION * gathered / diagonal
    for sweep_index in range(COARSE - 1):
        estimate = (
            estimate
            + RELAXATION * (gathered - block_operate_strip(estimate, offsets_now, coupling)) / diagonal
        )
    return lax.dynamic_slice_in_dim(estimate, lax.axis_index("gx") * columns, columns, 2)


def block_vcycle(residual, offsets_raw, layer_index):
    factor = 2**layer_index
    coupling = DIFFUSION / 4.0**layer_index
    diagonal = 1.0 + 4.0 * coupling + 2.0 * VERTICAL
    offsets_now = offsets_raw // factor
    if layer_index == LEVELS - 1:
        return block_coarsest(residual, offsets_now, coupling)
    estimate = RELAXATION * residual / diagonal
    defect = residual - block_operate(estimate, offsets_now, coupling)[0]
    planes, height, breadth = defect.shape
    coarser = defect.reshape(planes, height // 2, 2, breadth // 2, 2).mean(axis=(2, 4))
    correction = block_vcycle(coarser, offsets_raw, layer_index + 1)
    estimate = estimate + jnp.repeat(jnp.repeat(correction, 2, axis=1), 2, axis=2)
    estimate = (
        estimate + RELAXATION * (residual - block_operate(estimate, offsets_now, coupling)[0]) / diagonal
    )
    return estimate


def total_inner(first_field, second_field):
    return lax.psum(jnp.sum(first_field * second_field), ("gy", "gx"))


def spread(phase, velocity, offsets):
    phase_now = phase
    for time_step in range(STEPS):
        offsets_raw = offsets[time_step]
        applied, right_field, left_field = block_operate(phase_now, offsets_raw, DIFFUSION)
        source = (
            phase_now
            + REACTION * (phase_now - phase_now * phase_now * phase_now)
            - ADVECTION * velocity * (right_field - left_field)
        )
        residual = source - applied
        precond = block_vcycle(residual, offsets_raw, 0)
        projected = total_inner(residual, precond)
        direction = precond
        for iteration in range(ITERS):
            image = block_operate(direction, offsets_raw, DIFFUSION)[0]
            step_size = projected / total_inner(direction, image)
            phase_now = phase_now + step_size * direction
            residual = residual - step_size * image
            if iteration + 1 < ITERS:
                precond = block_vcycle(residual, offsets_raw, 0)
                following = total_inner(residual, precond)
                direction = precond + following / projected * direction
                projected = following
    return phase_now


MOST_DEVICES = 32
MOST_BYTES = 44 << 20


def local(phase, velocity, offsets):
    strips, width = lax.axis_size("gy"), lax.axis_size("gx")
    planes, rows, columns = phase.shape
    sizes = Level(0, width, rows, strips, planes).shape()
    fits = 8 * 4 * sizes[0] * sizes[1] < MOST_BYTES and strips * width <= MOST_DEVICES
    shaped = columns == LANES and rows % 32 == 0 and width in (8, 16, 32, 64) and strips % 4 == 0
    if fits and shaped:
        return on_whole(gathered(phase, velocity), offsets, strips, width)
    return spread(phase, velocity, offsets)


def solution(mesh):
    placed = (P(None, "gy", "gx"), P(None, "gy", "gx"), P())
    return jax.shard_map(local, mesh=mesh, in_specs=placed, out_specs=P(None, "gy", "gx"), check_vma=False)
```

```python
import jax
import jax.numpy as jnp
from jax import lax
from jax.experimental import pallas as pl
from jax.experimental.pallas import tpu as pltpu
from jax.sharding import PartitionSpec as P

STEPS = 2
ITERS = 2
LEVELS = 3
COARSE = 4

RELAXATION = 0.8
DIFFUSION = 4.0
VERTICAL = 1.0
REACTION = 0.5
ADVECTION = 0.5

LANES = 128
SUB = 8


class Level:
    def __init__(self, index, pages, strip_rows, strips, planes):
        self.pages = pages >> index
        self.rows = strip_rows >> index
        self.strips = strips
        self.planes = planes
        self.pitch = self.rows + SUB
        self.height = strips * self.pitch + SUB
        self.factor = 2**index
        self.coupling = DIFFUSION / 4.0**index
        self.diagonal = 1.0 + 4.0 * self.coupling + 2.0 * VERTICAL
        self.relax = RELAXATION / self.diagonal
        self.tiles = self.rows // SUB
        self.count = self.pages * planes

    def shape(self):
        return ((self.count + 2 * self.planes) * self.height, LANES)

    def base(self, strip, tile):
        row = SUB + strip * self.pitch + tile * SUB
        return row if isinstance(row, int) else pl.multiple_of(row, SUB)

    def at(self, page, plane, row):
        return ((page + 1) * self.planes + plane) * self.height + row


def tile_of(ref, level, page, plane, row):
    return ref[pl.ds(level.at(page, plane, row), SUB), :]


def put_tile(ref, level, page, plane, row, value):
    ref[pl.ds(level.at(page, plane, row), SUB), :] = value


def fill_halo(ref, level, offsets, step, halo):
    count, width = level.count, level.pages
    for strip in range(level.strips):
        for tile in range(level.tiles):
            for z in range(level.planes):
                row = level.base(strip, tile)
                put_tile(ref, level, width, z, row, pltpu.roll(tile_of(ref, level, 0, z, row), LANES - 1, 1))
                put_tile(ref, level, -1, z, row, pltpu.roll(tile_of(ref, level, width - 1, z, row), 1, 1))
    for strip in range(level.strips):
        shift = offsets[step, strip] // level.factor
        lane, page = shift // width, shift % width
        under = (strip - 1) % level.strips
        first = level.at(0, 0, SUB + strip * level.pitch)
        last = level.at(0, 0, SUB) + under * level.pitch + level.rows - 1
        upper = ref[pl.ds(first, count, stride=level.height), :]
        lower = ref[pl.ds(last, count, stride=level.height), :]
        start = strip * 4 * count
        halo[pl.ds(start, count), :] = pltpu.roll(upper, (LANES - lane) % LANES, 1)
        halo[pl.ds(start + count, count), :] = pltpu.roll(upper, LANES - 1 - lane, 1)
        halo[pl.ds(start + 2 * count, count), :] = pltpu.roll(lower, (lane + 1) % LANES, 1)
        halo[pl.ds(start + 3 * count, count), :] = pltpu.roll(lower, lane, 1)
        ref[pl.ds(last + 1, count, stride=level.height), :] = halo[pl.ds(start + page * level.planes, count), :]
        ref[pl.ds(first - 1, count, stride=level.height), :] = halo[
            pl.ds(start + 2 * count + (width - page) * level.planes, count), :
        ]


UNROLLED = 8


def repeat(count, body, carry):
    if count > UNROLLED:
        return lax.fori_loop(0, count, body, carry)
    for index in range(count):
        carry = body(index, carry)
    return carry


def stencil(ref, level, base):
    planes, width = level.planes, level.pages
    cell = [[tile_of(ref, level, p, z, base) for z in range(planes)] for p in range(-1, width + 1)]
    out = []
    for p in range(width):
        row = []
        for z in range(planes):
            left, here, right = cell[p][z], cell[p + 1][z], cell[p + 2][z]
            above = tile_of(ref, level, p, z, base + 1)
            below = tile_of(ref, level, p, z, base - 1)
            beside = (above + below) + (right + left)
            vertical = cell[p + 1][(z + 1) % planes] + cell[p + 1][(z - 1) % planes]
            row.append((here, right, left, beside, vertical))
        out.append(row)
    return out


def smooth(level, cell, beside, vertical):
    k = level.relax
    return (1.0 - k * level.diagonal) * cell + (k * level.coupling) * beside + (k * VERTICAL) * vertical


def apply(level, cell, beside, vertical):
    return level.diagonal * cell - level.coupling * beside - VERTICAL * vertical


def loop_coarse(coarse, body):
    count = coarse.strips * coarse.tiles
    if coarse.factor > 2:
        for index in range(count):
            body(index, 0)
    else:
        lax.fori_loop(0, count, body, 0)


def restrict(ref, level, coarse_ref, coarse, pairs):
    planes = level.planes

    def body(index, carry):
        strip, tile = index // coarse.tiles, index % coarse.tiles
        room = index * coarse.count * 2 * SUB if isinstance(index, int) else 0
        for half in range(2):
            base = level.base(strip, 2 * tile + half)
            terms = stencil(ref, level, base)
            for p in range(coarse.pages):
                for z in range(planes):
                    total = 0.0
                    for q in (2 * p, 2 * p + 1):
                        cell, _, _, beside, vertical = terms[q][z]
                        total = total + smooth(level, cell, beside, vertical)
                    pairs[pl.ds(room + (p * planes + z) * 2 * SUB + half * SUB, SUB), :] = total
        for p in range(coarse.pages):
            for z in range(planes):
                start = room + (p * planes + z) * 2 * SUB
                even = pairs[pl.ds(start, SUB, stride=2), :]
                odd = pairs[pl.ds(start + 1, SUB, stride=2), :]
                put_tile(coarse_ref, coarse, p, z, coarse.base(strip, tile), 0.25 * (even + odd))
        return carry

    loop_coarse(coarse, body)


def prolong(coarse_ref, coarse, residual, level, ref, pairs):
    planes = level.planes

    def body(index, carry):
        strip, tile = index // coarse.tiles, index % coarse.tiles
        room = index * coarse.count * 2 * SUB if isinstance(index, int) else 0
        for p in range(coarse.pages):
            for z in range(planes):
                start = room + (p * planes + z) * 2 * SUB
                value = tile_of(coarse_ref, coarse, p, z, coarse.base(strip, tile))
                pairs[pl.ds(start, SUB, stride=2), :] = value
                pairs[pl.ds(start + 1, SUB, stride=2), :] = value
        for p in range(coarse.pages):
            for z in range(planes):
                start = room + (p * planes + z) * 2 * SUB
                for half in range(2):
                    value = pairs[pl.ds(start + half * SUB, SUB), :]
                    base = level.base(strip, 2 * tile + half)
                    for q in (2 * p, 2 * p + 1):
                        put_tile(ref, level, q, z, base, level.relax * tile_of(residual, level, q, z, base) + value)
        return carry

    loop_coarse(coarse, body)


def per_tile(level, body, sums):
    def step(index, carry):
        return body(level.base(index // level.tiles, index % level.tiles), carry)

    zero = jnp.zeros((SUB, LANES), jnp.float32)
    return repeat(level.strips * level.tiles, step, (zero,) * sums)


def total(vector):
    return jnp.sum(jnp.sum(vector, axis=0, keepdims=True), axis=1, keepdims=True)


def relaxed(ref, residual, level, target):
    def body(base, carry):
        for p, row in enumerate(stencil(ref, level, base)):
            for z, (cell, _, _, beside, vertical) in enumerate(row):
                value = smooth(level, cell, beside, vertical) + level.relax * tile_of(residual, level, p, z, base)
                put_tile(target, level, p, z, base, value)
        return carry

    per_tile(level, body, 0)


def coarsest(residual, level, offsets, step, spare, halo):
    def first(base, carry):
        for p, row in enumerate(stencil(residual, level, base)):
            for z, (cell, _, _, beside, vertical) in enumerate(row):
                put_tile(spare[0], level, p, z, base, level.relax * (cell + smooth(level, cell, beside, vertical)))
        return carry

    fill_halo(residual, level, offsets, step, halo)
    per_tile(level, first, 0)
    now = 0
    for _ in range(COARSE - 2):
        fill_halo(spare[now], level, offsets, step, halo)
        relaxed(spare[now], residual, level, spare[1 - now])
        now = 1 - now
    return spare[now]


def vcycle(residual, levels, index, offsets, step, work, halo, pairs):
    level, coarse = levels[index], levels[index + 1]
    below, estimate = work[index + 1], work[index][1]
    fill_halo(residual, level, offsets, step, halo)
    restrict(residual, level, below[0], coarse, pairs)
    if index + 2 == LEVELS:
        correction = coarsest(below[0], coarse, offsets, step, below[1:], halo)
    else:
        vcycle(below[0], levels, index + 1, offsets, step, work, halo, pairs)
        correction = below[2]
        relaxed(below[1], below[0], coarse, correction)
    prolong(correction, coarse, residual, level, estimate, pairs)
    fill_halo(estimate, level, offsets, step, halo)


def interleave(blocks, dy_count, level, gy, gx, targets, stage):
    width, planes = level.pages, level.planes
    lane = lax.broadcasted_iota(jnp.int32, (SUB, LANES), 1)
    per = LANES // width
    source = (lane % per) * width + lane // per
    groups = [
        (name, dy, z, tile) for name in range(len(targets)) for dy in range(dy_count) for z in range(planes) for tile in range(level.tiles)
    ]

    def slot(turn, group, page):
        return pl.ds(((turn % 2 * len(groups) + group) * width + page) * SUB, SUB)

    bits = [1 << i for i in range(width.bit_length() - 1)]
    for turn, bit in enumerate(bits):
        mine = (gx // bit) % 2
        keep = (lane // bit + mine) % 2 == 0
        shift = jnp.where(mine == 0, bit, LANES - bit)
        for group, (name, dy, z, tile) in enumerate(groups):
            for p in range(width):
                if p & bit:
                    continue
                if turn == 0:
                    a, b = (blocks(name, dy, q, z, tile) for q in (p, p | bit))
                else:
                    a, b = (stage[slot(turn, group, q), :] for q in (p, p | bit))
                stage[slot(turn + 1, group, p), :] = jnp.where(keep, a, pltpu.roll(b, shift, 1))
                stage[slot(turn + 1, group, p | bit), :] = jnp.where(keep, pltpu.roll(a, LANES - shift, 1), b)
    for group, (name, dy, z, tile) in enumerate(groups):
        row = level.base(jnp.bitwise_xor(gy, dy), tile)
        for p in range(width):
            value = jnp.take_along_axis(stage[slot(len(bits), group, p), :], source, axis=1)
            put_tile(targets[name], level, jnp.bitwise_xor(gx, p), z, row, value)


def solve(offsets, u, v, r, q, w, work, halo, pairs, levels):
    fine = levels[0]
    e = work[0][1]
    update = None
    for step in range(STEPS):
        fill_halo(u, fine, offsets, step, halo)

        def residual(base, carry):
            for p, row in enumerate(stencil(u, fine, base)):
                for z, (cell, right, left, beside, vertical) in enumerate(row):
                    speed = tile_of(v, fine, p, z, base)
                    cube = cell * cell * cell
                    value = (
                        (1.0 + REACTION - fine.diagonal) * cell
                        - REACTION * cube
                        - ADVECTION * speed * (right - left)
                        + fine.coupling * beside
                        + VERTICAL * vertical
                    )
                    put_tile(r, fine, p, z, base, value)
            return carry

        per_tile(fine, residual, 0)
        vcycle(r, levels, 0, offsets, step, work, halo, pairs)

        def finish(base, carry):
            (rw,) = carry
            for p, row in enumerate(stencil(e, fine, base)):
                for z, (cell, _, _, beside, vertical) in enumerate(row):
                    res = tile_of(r, fine, p, z, base)
                    value = smooth(fine, cell, beside, vertical) + fine.relax * res
                    put_tile(w, fine, p, z, base, value)
                    rw = rw + res * value
            return (rw,)

        (rw,) = per_tile(fine, finish, 1)
        rw = total(rw)
        fill_halo(w, fine, offsets, step, halo)

        def image(base, carry):
            (wq,) = carry
            for p, row in enumerate(stencil(w, fine, base)):
                for z, (cell, _, _, beside, vertical) in enumerate(row):
                    value = apply(fine, cell, beside, vertical)
                    put_tile(q, fine, p, z, base, value)
                    wq = wq + cell * value
            return (wq,)

        (wq,) = per_tile(fine, image, 1)
        alpha = rw / total(wq)
        vcycle(q, levels, 0, offsets, step, work, halo, pairs)

        def finish_next(base, carry):
            (rw,) = carry
            for p, row in enumerate(stencil(e, fine, base)):
                for z, (cell, _, _, beside, vertical) in enumerate(row):
                    img = tile_of(q, fine, p, z, base)
                    value = smooth(fine, cell, beside, vertical) + fine.relax * img
                    res = tile_of(r, fine, p, z, base) - alpha * img
                    value = tile_of(w, fine, p, z, base) - alpha * value
                    put_tile(r, fine, p, z, base, value)
                    rw = rw + res * value
            return (rw,)

        (following,) = per_tile(fine, finish_next, 1)
        following = total(following)
        beta = following / rw
        fill_halo(r, fine, offsets, step, halo)

        def image_next(base, carry):
            (pq,) = carry
            for p, row in enumerate(stencil(r, fine, base)):
                for z, (cell, _, _, beside, vertical) in enumerate(row):
                    direction = cell + beta * tile_of(w, fine, p, z, base)
                    value = apply(fine, cell, beside, vertical) + beta * tile_of(q, fine, p, z, base)
                    pq = pq + direction * value
            return (pq,)

        (pq,) = per_tile(fine, image_next, 1)
        alpha_next = following / total(pq)
        along = alpha + alpha_next * beta

        def update(base, carry):
            for p in range(fine.pages):
                for z in range(fine.planes):
                    value = (
                        tile_of(u, fine, p, z, base)
                        + along * tile_of(w, fine, p, z, base)
                        + alpha_next * tile_of(r, fine, p, z, base)
                    )
                    put_tile(u, fine, p, z, base, value)
            return carry

        if step + 1 < STEPS:
            per_tile(fine, update, 0)
    return update


def whole_kernel(places, arrays, levels, *refs):
    offsets, held, out = refs[0], refs[1 : 1 + arrays], refs[1 + arrays]
    u, v, r, q, w, e, r1, e1, f1, r2, e2, f2, halo, pairs, stage = refs[2 + arrays :]
    fine = levels[0]
    gy, gx = lax.axis_index("gy"), lax.axis_index("gx")

    def block(name, dy, dx, z, tile):
        array, place = places[dy, dx]
        return held[array][place, name, z, pl.ds(tile * SUB, SUB), :]

    interleave(block, fine.strips, fine, gy, gx, (u, v), stage)
    work = [[r, e], [r1, e1, f1], [r2, e2, f2]]
    update = solve(offsets, u, v, r, q, w, work, halo, pairs, levels)
    lane = lax.broadcasted_iota(jnp.int32, (SUB, LANES), 1)
    source = gx * (LANES // fine.pages) + lane // fine.pages
    for tile in range(fine.tiles):
        base = fine.base(gy, tile)
        update(base, ())
        for z in range(fine.planes):
            value = jnp.zeros((SUB, LANES), jnp.float32)
            for p in range(fine.pages):
                page = jnp.take_along_axis(tile_of(u, fine, p, z, base), source, axis=1)
                value = jnp.where(lane % fine.pages == p, page, value)
            out[z, pl.ds(tile * SUB, SUB), :] = value


def on_whole(arrays, places, offsets, strips, width):
    _, _, planes, rows, columns = arrays[0].shape
    levels = [Level(i, width, rows, strips, planes) for i in range(LEVELS)]
    fields = [pltpu.VMEM(levels[0].shape(), jnp.float32)] * 6
    fields += [pltpu.VMEM(levels[1].shape(), jnp.float32)] * 3 + [pltpu.VMEM(levels[2].shape(), jnp.float32)] * 3
    count = levels[0].count
    scratch = fields + [
        pltpu.VMEM((strips * 4 * count, LANES), jnp.float32),
        pltpu.VMEM((count * SUB * 2, LANES), jnp.float32),
        pltpu.VMEM((2 * 2 * planes * strips * rows * width, LANES), jnp.float32),
    ]

    def kernel(*refs):
        whole_kernel(places, len(arrays), levels, *refs)

    return pl.pallas_call(
        kernel,
        out_shape=jax.ShapeDtypeStruct((planes, rows, columns), jnp.float32),
        in_specs=[pl.BlockSpec(memory_space=pltpu.SMEM)] + [pl.BlockSpec(memory_space=pltpu.VMEM)] * len(arrays),
        out_specs=pl.BlockSpec(memory_space=pltpu.VMEM),
        scratch_shapes=scratch,
        compiler_params=pltpu.CompilerParams(vmem_limit_bytes=48 << 20),
    )(offsets, *arrays)


def swapped(block, axis, bits):
    count = lax.axis_size(axis)
    return lax.ppermute(block, axis, [(i, i ^ bits) for i in range(count)])


def gathered(phase, velocity):
    width = lax.axis_size("gx")
    own = jnp.stack([phase, velocity])[None]
    steps = list(range(0, width, 2))
    half = len(steps) // 2
    line = jnp.concatenate([own] + [swapped(own, "gx", k) for k in steps[1:]])
    across = swapped(line, "gx", 1)
    along = swapped(line, "gy", 2)
    corner = [swapped(across[:half], "gy", 2), swapped(along[half:], "gx", 1)]
    arrays = [line, across, along] + corner
    arrays += [swapped(array, "gy", 1) for array in arrays]
    places = {}
    for core in range(2):
        for i, k in enumerate(steps):
            for dy, dx, array, place in (
                (0, 0, 0, i),
                (0, 1, 1, i),
                (2, 0, 2, i),
                (2, 1, 3 if i < half else 4, i % half),
            ):
                places[dy ^ core, dx ^ k] = (array + 5 * core, place)
    return arrays, places


def padded(cells, sides, width):
    for axis, dim in sides:
        count = lax.axis_size(axis)
        head = lax.slice_in_dim(cells, 0, width, axis=dim)
        tail = lax.slice_in_dim(cells, cells.shape[dim] - width, cells.shape[dim], axis=dim)
        cells = jnp.concatenate(
            [
                lax.ppermute(tail, axis, [(i, (i + 1) % count) for i in range(count)]),
                cells,
                lax.ppermute(head, axis, [((i + 1) % count, i) for i in range(count)]),
            ],
            axis=dim,
        )
    return cells


def sheared(bottom_row, upper_row, offsets_now, anchor, columns):
    breadth = bottom_row.shape[1]
    device_row = lax.axis_index("gy")
    row_count = lax.axis_size("gy")
    below_shift = offsets_now[device_row]
    above_shift = offsets_now[(device_row + 1) % row_count]
    local_columns = jnp.arange(columns, dtype=jnp.int32)
    down_index = (anchor + below_shift + local_columns) % breadth
    up_index = (anchor - above_shift + local_columns) % breadth
    down_window = jnp.take(bottom_row, down_index, axis=1)
    up_window = jnp.take(upper_row, up_index, axis=1)
    stacked = jnp.stack([down_window, up_window], axis=1)
    rims = padded(stacked, (("gy", 1),), 1)
    return (rims[:, 0, :], rims[:, 3, :])


def block_stencil(field, below_row, above_row, across, coupling):
    diagonal = 1.0 + 4.0 * coupling + 2.0 * VERTICAL
    column_pad = jnp.concatenate([below_row[:, None, :], field, above_row[:, None, :]], axis=1)
    beside = column_pad[:, 2:, :] + column_pad[:, :-2, :] + across
    vertical_sum = jnp.roll(field, 1, 0) + jnp.roll(field, -1, 0)
    return diagonal * field - coupling * beside - VERTICAL * vertical_sum


def block_operate(field, offsets_now, coupling):
    columns = field.shape[2]
    margins = padded(field, (("gx", 2),), 1)
    bottom_full, upper_full = (
        lax.all_gather(field[:, 0, :], "gx", axis=1, tiled=True),
        lax.all_gather(field[:, -1, :], "gx", axis=1, tiled=True),
    )
    right_field = margins[:, :, 2:]
    left_field = margins[:, :, :-2]
    below_row, above_row = sheared(
        bottom_full, upper_full, offsets_now, lax.axis_index("gx") * columns, columns
    )
    across = right_field + left_field
    return (block_stencil(field, below_row, above_row, across, coupling), right_field, left_field)


def block_operate_strip(field, offsets_now, coupling):
    below_row, above_row = sheared(field[:, 0, :], field[:, -1, :], offsets_now, 0, field.shape[2])
    across = jnp.roll(field, 1, 2) + jnp.roll(field, -1, 2)
    return block_stencil(field, below_row, above_row, across, coupling)


def block_coarsest(residual, offsets_now, coupling):
    diagonal = 1.0 + 4.0 * coupling + 2.0 * VERTICAL
    columns = residual.shape[2]
    gathered = lax.all_gather(residual, "gx", axis=2, tiled=True)
    estimate = RELAXATION * gathered / diagonal
    for sweep_index in range(COARSE - 1):
        estimate = (
            estimate
            + RELAXATION * (gathered - block_operate_strip(estimate, offsets_now, coupling)) / diagonal
        )
    return lax.dynamic_slice_in_dim(estimate, lax.axis_index("gx") * columns, columns, 2)


def block_vcycle(residual, offsets_raw, layer_index):
    factor = 2**layer_index
    coupling = DIFFUSION / 4.0**layer_index
    diagonal = 1.0 + 4.0 * coupling + 2.0 * VERTICAL
    offsets_now = offsets_raw // factor
    if layer_index == LEVELS - 1:
        return block_coarsest(residual, offsets_now, coupling)
    estimate = RELAXATION * residual / diagonal
    defect = residual - block_operate(estimate, offsets_now, coupling)[0]
    planes, height, breadth = defect.shape
    coarser = defect.reshape(planes, height // 2, 2, breadth // 2, 2).mean(axis=(2, 4))
    correction = block_vcycle(coarser, offsets_raw, layer_index + 1)
    estimate = estimate + jnp.repeat(jnp.repeat(correction, 2, axis=1), 2, axis=2)
    estimate = (
        estimate + RELAXATION * (residual - block_operate(estimate, offsets_now, coupling)[0]) / diagonal
    )
    return estimate


def total_inner(first_field, second_field):
    return lax.psum(jnp.sum(first_field * second_field), ("gy", "gx"))


def spread(phase, velocity, offsets):
    phase_now = phase
    for time_step in range(STEPS):
        offsets_raw = offsets[time_step]
        applied, right_field, left_field = block_operate(phase_now, offsets_raw, DIFFUSION)
        source = (
            phase_now
            + REACTION * (phase_now - phase_now * phase_now * phase_now)
            - ADVECTION * velocity * (right_field - left_field)
        )
        residual = source - applied
        precond = block_vcycle(residual, offsets_raw, 0)
        projected = total_inner(residual, precond)
        direction = precond
        for iteration in range(ITERS):
            image = block_operate(direction, offsets_raw, DIFFUSION)[0]
            step_size = projected / total_inner(direction, image)
            phase_now = phase_now + step_size * direction
            residual = residual - step_size * image
            if iteration + 1 < ITERS:
                precond = block_vcycle(residual, offsets_raw, 0)
                following = total_inner(residual, precond)
                direction = precond + following / projected * direction
                projected = following
    return phase_now


MOST_DEVICES = 32
MOST_BYTES = 44 << 20


def local(phase, velocity, offsets):
    strips, width = lax.axis_size("gy"), lax.axis_size("gx")
    planes, rows, columns = phase.shape
    sizes = Level(0, width, rows, strips, planes).shape()
    fits = 10 * 4 * sizes[0] * sizes[1] < MOST_BYTES and strips * width <= MOST_DEVICES
    shaped = columns == LANES and rows % 32 == 0 and width in (8, 16, 32, 64) and strips == 4
    if fits and shaped:
        return on_whole(*gathered(phase, velocity), offsets, strips, width)
    return spread(phase, velocity, offsets)


def solution(mesh):
    placed = (P(None, "gy", "gx"), P(None, "gy", "gx"), P())
    return jax.shard_map(local, mesh=mesh, in_specs=placed, out_specs=P(None, "gy", "gx"), check_vma=False)
```

```python
import jax
import jax.numpy as jnp
from jax import lax
from jax.experimental import pallas as pl
from jax.experimental.pallas import tpu as pltpu
from jax.sharding import PartitionSpec as P

STEPS = 2
ITERS = 2
LEVELS = 3
COARSE = 4

RELAXATION = 0.8
DIFFUSION = 4.0
VERTICAL = 1.0
REACTION = 0.5
ADVECTION = 0.5

LANES = 128
SUB = 8


class Level:
    def __init__(self, index, pages, strip_rows, strips, planes):
        self.pages = pages >> index
        self.rows = strip_rows >> index
        self.strips = strips
        self.planes = planes
        self.pitch = self.rows + SUB
        self.height = strips * self.pitch + SUB
        self.factor = 2**index
        self.coupling = DIFFUSION / 4.0**index
        self.diagonal = 1.0 + 4.0 * self.coupling + 2.0 * VERTICAL
        self.relax = RELAXATION / self.diagonal
        self.tiles = self.rows // SUB
        self.count = self.pages * planes

    def shape(self):
        return ((self.count + 2 * self.planes) * self.height, LANES)

    def base(self, strip, tile):
        row = SUB + strip * self.pitch + tile * SUB
        return row if isinstance(row, int) else pl.multiple_of(row, SUB)

    def at(self, page, plane, row):
        return ((page + 1) * self.planes + plane) * self.height + row


def tile_of(ref, level, page, plane, row):
    return ref[pl.ds(level.at(page, plane, row), SUB), :]


def put_tile(ref, level, page, plane, row, value):
    ref[pl.ds(level.at(page, plane, row), SUB), :] = value


def fill_halo(ref, level, offsets, step, halo):
    count, width = level.count, level.pages
    for strip in range(level.strips):
        for tile in range(level.tiles):
            for z in range(level.planes):
                row = level.base(strip, tile)
                put_tile(ref, level, width, z, row, pltpu.roll(tile_of(ref, level, 0, z, row), LANES - 1, 1))
                put_tile(ref, level, -1, z, row, pltpu.roll(tile_of(ref, level, width - 1, z, row), 1, 1))
    for strip in range(level.strips):
        shift = offsets[step, strip] // level.factor
        lane, page = shift // width, shift % width
        under = (strip - 1) % level.strips
        first = level.at(0, 0, SUB + strip * level.pitch)
        last = level.at(0, 0, SUB) + under * level.pitch + level.rows - 1
        upper = ref[pl.ds(first, count, stride=level.height), :]
        lower = ref[pl.ds(last, count, stride=level.height), :]
        start = strip * 4 * count
        halo[pl.ds(start, count), :] = pltpu.roll(upper, (LANES - lane) % LANES, 1)
        halo[pl.ds(start + count, count), :] = pltpu.roll(upper, LANES - 1 - lane, 1)
        halo[pl.ds(start + 2 * count, count), :] = pltpu.roll(lower, (lane + 1) % LANES, 1)
        halo[pl.ds(start + 3 * count, count), :] = pltpu.roll(lower, lane, 1)
        ref[pl.ds(last + 1, count, stride=level.height), :] = halo[pl.ds(start + page * level.planes, count), :]
        ref[pl.ds(first - 1, count, stride=level.height), :] = halo[
            pl.ds(start + 2 * count + (width - page) * level.planes, count), :
        ]


UNROLLED = 16


def repeat(count, body, carry):
    if count > UNROLLED:
        return lax.fori_loop(0, count, body, carry)
    for index in range(count):
        carry = body(index, carry)
    return carry


def stencil(ref, level, base):
    planes, width = level.planes, level.pages
    cell = [[tile_of(ref, level, p, z, base) for z in range(planes)] for p in range(-1, width + 1)]
    out = []
    for p in range(width):
        row = []
        for z in range(planes):
            left, here, right = cell[p][z], cell[p + 1][z], cell[p + 2][z]
            above = tile_of(ref, level, p, z, base + 1)
            below = tile_of(ref, level, p, z, base - 1)
            beside = (above + below) + (right + left)
            vertical = cell[p + 1][(z + 1) % planes] + cell[p + 1][(z - 1) % planes]
            row.append((here, right, left, beside, vertical))
        out.append(row)
    return out


def smooth(level, cell, beside, vertical):
    k = level.relax
    return (1.0 - k * level.diagonal) * cell + (k * level.coupling) * beside + (k * VERTICAL) * vertical


def apply(level, cell, beside, vertical):
    return level.diagonal * cell - level.coupling * beside - VERTICAL * vertical


def loop_coarse(coarse, body):
    count = coarse.strips * coarse.tiles
    if count <= 16:
        for index in range(count):
            body(index, 0)
    else:
        lax.fori_loop(0, count, body, 0)


def restrict(ref, level, coarse_ref, coarse, pairs):
    planes = level.planes

    def body(index, carry):
        strip, tile = index // coarse.tiles, index % coarse.tiles
        room = index * coarse.count * 2 * SUB if isinstance(index, int) else 0
        for half in range(2):
            base = level.base(strip, 2 * tile + half)
            terms = stencil(ref, level, base)
            for p in range(coarse.pages):
                for z in range(planes):
                    total = 0.0
                    for q in (2 * p, 2 * p + 1):
                        cell, _, _, beside, vertical = terms[q][z]
                        total = total + smooth(level, cell, beside, vertical)
                    pairs[pl.ds(room + (p * planes + z) * 2 * SUB + half * SUB, SUB), :] = total
        for p in range(coarse.pages):
            for z in range(planes):
                start = room + (p * planes + z) * 2 * SUB
                even = pairs[pl.ds(start, SUB, stride=2), :]
                odd = pairs[pl.ds(start + 1, SUB, stride=2), :]
                put_tile(coarse_ref, coarse, p, z, coarse.base(strip, tile), 0.25 * (even + odd))
        return carry

    loop_coarse(coarse, body)


def prolong(coarse_ref, coarse, residual, level, ref, pairs):
    planes = level.planes

    def body(index, carry):
        strip, tile = index // coarse.tiles, index % coarse.tiles
        room = index * coarse.count * 2 * SUB if isinstance(index, int) else 0
        for p in range(coarse.pages):
            for z in range(planes):
                start = room + (p * planes + z) * 2 * SUB
                value = tile_of(coarse_ref, coarse, p, z, coarse.base(strip, tile))
                pairs[pl.ds(start, SUB, stride=2), :] = value
                pairs[pl.ds(start + 1, SUB, stride=2), :] = value
        for p in range(coarse.pages):
            for z in range(planes):
                start = room + (p * planes + z) * 2 * SUB
                for half in range(2):
                    value = pairs[pl.ds(start + half * SUB, SUB), :]
                    base = level.base(strip, 2 * tile + half)
                    for q in (2 * p, 2 * p + 1):
                        put_tile(ref, level, q, z, base, level.relax * tile_of(residual, level, q, z, base) + value)
        return carry

    loop_coarse(coarse, body)


def per_tile(level, body, sums):
    def step(index, carry):
        return body(level.base(index // level.tiles, index % level.tiles), carry)

    zero = jnp.zeros((SUB, LANES), jnp.float32)
    return repeat(level.strips * level.tiles, step, (zero,) * sums)


def total(vector):
    return jnp.sum(jnp.sum(vector, axis=0, keepdims=True), axis=1, keepdims=True)


def relaxed(ref, residual, level, target):
    def body(base, carry):
        for p, row in enumerate(stencil(ref, level, base)):
            for z, (cell, _, _, beside, vertical) in enumerate(row):
                value = smooth(level, cell, beside, vertical) + level.relax * tile_of(residual, level, p, z, base)
                put_tile(target, level, p, z, base, value)
        return carry

    per_tile(level, body, 0)


def coarsest(residual, level, offsets, step, spare, halo):
    def first(base, carry):
        for p, row in enumerate(stencil(residual, level, base)):
            for z, (cell, _, _, beside, vertical) in enumerate(row):
                put_tile(spare[0], level, p, z, base, level.relax * (cell + smooth(level, cell, beside, vertical)))
        return carry

    fill_halo(residual, level, offsets, step, halo)
    per_tile(level, first, 0)
    now = 0
    for _ in range(COARSE - 2):
        fill_halo(spare[now], level, offsets, step, halo)
        relaxed(spare[now], residual, level, spare[1 - now])
        now = 1 - now
    return spare[now]


def vcycle(residual, levels, index, offsets, step, work, halo, pairs):
    level, coarse = levels[index], levels[index + 1]
    below, estimate = work[index + 1], work[index][1]
    fill_halo(residual, level, offsets, step, halo)
    restrict(residual, level, below[0], coarse, pairs)
    if index + 2 == LEVELS:
        correction = coarsest(below[0], coarse, offsets, step, below[1:], halo)
    else:
        vcycle(below[0], levels, index + 1, offsets, step, work, halo, pairs)
        correction = below[2]
        relaxed(below[1], below[0], coarse, correction)
    prolong(correction, coarse, residual, level, estimate, pairs)
    fill_halo(estimate, level, offsets, step, halo)


def interleave(blocks, dy_count, level, gy, gx, targets, stage):
    width, planes = level.pages, level.planes
    lane = lax.broadcasted_iota(jnp.int32, (SUB, LANES), 1)
    per = LANES // width
    source = (lane % per) * width + lane // per
    groups = [
        (name, dy, z, tile) for name in range(len(targets)) for dy in range(dy_count) for z in range(planes) for tile in range(level.tiles)
    ]

    def slot(turn, group, page):
        return pl.ds(((turn % 2 * len(groups) + group) * width + page) * SUB, SUB)

    bits = [1 << i for i in range(width.bit_length() - 1)]
    for turn, bit in enumerate(bits):
        mine = (gx // bit) % 2
        keep = (lane // bit + mine) % 2 == 0
        shift = jnp.where(mine == 0, bit, LANES - bit)
        for group, (name, dy, z, tile) in enumerate(groups):
            for p in range(width):
                if p & bit:
                    continue
                if turn == 0:
                    a, b = (blocks(name, dy, q, z, tile) for q in (p, p | bit))
                else:
                    a, b = (stage[slot(turn, group, q), :] for q in (p, p | bit))
                stage[slot(turn + 1, group, p), :] = jnp.where(keep, a, pltpu.roll(b, shift, 1))
                stage[slot(turn + 1, group, p | bit), :] = jnp.where(keep, pltpu.roll(a, LANES - shift, 1), b)
    for group, (name, dy, z, tile) in enumerate(groups):
        row = level.base(jnp.bitwise_xor(gy, dy), tile)
        for p in range(width):
            value = jnp.take_along_axis(stage[slot(len(bits), group, p), :], source, axis=1)
            put_tile(targets[name], level, jnp.bitwise_xor(gx, p), z, row, value)


def solve(offsets, u, v, r, q, w, work, halo, pairs, levels):
    fine = levels[0]
    e = work[0][1]
    update = None
    for step in range(STEPS):
        fill_halo(u, fine, offsets, step, halo)

        def residual(base, carry):
            for p, row in enumerate(stencil(u, fine, base)):
                for z, (cell, right, left, beside, vertical) in enumerate(row):
                    speed = tile_of(v, fine, p, z, base)
                    cube = cell * cell * cell
                    value = (
                        (1.0 + REACTION - fine.diagonal) * cell
                        - REACTION * cube
                        - ADVECTION * speed * (right - left)
                        + fine.coupling * beside
                        + VERTICAL * vertical
                    )
                    put_tile(r, fine, p, z, base, value)
            return carry

        per_tile(fine, residual, 0)
        vcycle(r, levels, 0, offsets, step, work, halo, pairs)

        def finish(base, carry):
            (rw,) = carry
            for p, row in enumerate(stencil(e, fine, base)):
                for z, (cell, _, _, beside, vertical) in enumerate(row):
                    res = tile_of(r, fine, p, z, base)
                    value = smooth(fine, cell, beside, vertical) + fine.relax * res
                    put_tile(w, fine, p, z, base, value)
                    rw = rw + res * value
            return (rw,)

        (rw,) = per_tile(fine, finish, 1)
        rw = total(rw)
        fill_halo(w, fine, offsets, step, halo)

        def image(base, carry):
            (wq,) = carry
            for p, row in enumerate(stencil(w, fine, base)):
                for z, (cell, _, _, beside, vertical) in enumerate(row):
                    value = apply(fine, cell, beside, vertical)
                    put_tile(q, fine, p, z, base, value)
                    wq = wq + cell * value
            return (wq,)

        (wq,) = per_tile(fine, image, 1)
        alpha = rw / total(wq)
        vcycle(q, levels, 0, offsets, step, work, halo, pairs)

        def finish_next(base, carry):
            (rw,) = carry
            for p, row in enumerate(stencil(e, fine, base)):
                for z, (cell, _, _, beside, vertical) in enumerate(row):
                    img = tile_of(q, fine, p, z, base)
                    value = smooth(fine, cell, beside, vertical) + fine.relax * img
                    res = tile_of(r, fine, p, z, base) - alpha * img
                    value = tile_of(w, fine, p, z, base) - alpha * value
                    put_tile(r, fine, p, z, base, value)
                    rw = rw + res * value
            return (rw,)

        (following,) = per_tile(fine, finish_next, 1)
        following = total(following)
        beta = following / rw
        fill_halo(r, fine, offsets, step, halo)

        def image_next(base, carry):
            (pq,) = carry
            for p, row in enumerate(stencil(r, fine, base)):
                for z, (cell, _, _, beside, vertical) in enumerate(row):
                    direction = cell + beta * tile_of(w, fine, p, z, base)
                    value = apply(fine, cell, beside, vertical) + beta * tile_of(q, fine, p, z, base)
                    pq = pq + direction * value
            return (pq,)

        (pq,) = per_tile(fine, image_next, 1)
        alpha_next = following / total(pq)
        along = alpha + alpha_next * beta

        def update(base, carry):
            for p in range(fine.pages):
                for z in range(fine.planes):
                    value = (
                        tile_of(u, fine, p, z, base)
                        + along * tile_of(w, fine, p, z, base)
                        + alpha_next * tile_of(r, fine, p, z, base)
                    )
                    put_tile(u, fine, p, z, base, value)
            return carry

        if step + 1 < STEPS:
            per_tile(fine, update, 0)
    return update


def whole_kernel(places, arrays, levels, *refs):
    offsets, held, out = refs[0], refs[1 : 1 + arrays], refs[1 + arrays]
    u, v, r, q, w, e, r1, e1, f1, r2, e2, f2, halo, pairs, stage = refs[2 + arrays :]
    fine = levels[0]
    gy, gx = lax.axis_index("gy"), lax.axis_index("gx")

    def block(name, dy, dx, z, tile):
        array, place = places[name, dy, dx]
        return held[array][(*place, z, pl.ds(tile * SUB, SUB), slice(None))]

    interleave(block, fine.strips, fine, gy, gx, (u, v), stage)
    work = [[r, e], [r1, e1, f1], [r2, e2, f2]]
    update = solve(offsets, u, v, r, q, w, work, halo, pairs, levels)
    lane = lax.broadcasted_iota(jnp.int32, (SUB, LANES), 1)
    source = gx * (LANES // fine.pages) + lane // fine.pages
    for tile in range(fine.tiles):
        base = fine.base(gy, tile)
        update(base, ())
        for z in range(fine.planes):
            value = jnp.zeros((SUB, LANES), jnp.float32)
            for p in range(fine.pages):
                page = jnp.take_along_axis(tile_of(u, fine, p, z, base), source, axis=1)
                value = jnp.where(lane % fine.pages == p, page, value)
            out[z, pl.ds(tile * SUB, SUB), :] = value


def on_whole(arrays, places, offsets, strips, width):
    planes, rows, columns = arrays[0].shape[-3:]
    levels = [Level(i, width, rows, strips, planes) for i in range(LEVELS)]
    fields = [pltpu.VMEM(levels[0].shape(), jnp.float32)] * 6
    fields += [pltpu.VMEM(levels[1].shape(), jnp.float32)] * 3 + [pltpu.VMEM(levels[2].shape(), jnp.float32)] * 3
    count = levels[0].count
    scratch = fields + [
        pltpu.VMEM((strips * 4 * count, LANES), jnp.float32),
        pltpu.VMEM((planes * strips * rows * width // 2, LANES), jnp.float32),
        pltpu.VMEM((2 * 2 * planes * strips * rows * width, LANES), jnp.float32),
    ]

    def kernel(*refs):
        whole_kernel(places, len(arrays), levels, *refs)

    return pl.pallas_call(
        kernel,
        out_shape=jax.ShapeDtypeStruct((planes, rows, columns), jnp.float32),
        in_specs=[pl.BlockSpec(memory_space=pltpu.SMEM)] + [pl.BlockSpec(memory_space=pltpu.VMEM)] * len(arrays),
        out_specs=pl.BlockSpec(memory_space=pltpu.VMEM),
        scratch_shapes=scratch,
        compiler_params=pltpu.CompilerParams(vmem_limit_bytes=48 << 20),
    )(offsets, *arrays)


def swapped(block, axis, bits):
    count = lax.axis_size(axis)
    return lax.ppermute(block, axis, [(i, i ^ bits) for i in range(count)])


def gathered(phase, velocity):
    width = lax.axis_size("gx")
    steps = list(range(0, width, 2))
    arrays, places = [], {}
    for name, own in enumerate((phase, velocity)):
        own = own[None]
        got = {k: swapped(own, "gx", k) for k in steps[1:]}
        line = jnp.concatenate([own] + [got[k] for k in steps[1:]])
        across = swapped(line, "gx", 1)
        along = swapped(line, "gy", 2)
        corner = swapped(along, "gx", 1) if name else swapped(across, "gy", 2)
        for dy, dx, array in ((0, 0, line), (0, 1, across), (2, 0, along), (2, 1, corner)):
            for core in range(2):
                for i, k in enumerate(steps):
                    places[name, dy ^ core, dx ^ k] = (len(arrays), (i,))
                arrays.append(swapped(array, "gy", 1) if core else array)
    return arrays, places


def padded(cells, sides, width):
    for axis, dim in sides:
        count = lax.axis_size(axis)
        head = lax.slice_in_dim(cells, 0, width, axis=dim)
        tail = lax.slice_in_dim(cells, cells.shape[dim] - width, cells.shape[dim], axis=dim)
        cells = jnp.concatenate(
            [
                lax.ppermute(tail, axis, [(i, (i + 1) % count) for i in range(count)]),
                cells,
                lax.ppermute(head, axis, [((i + 1) % count, i) for i in range(count)]),
            ],
            axis=dim,
        )
    return cells


def sheared(bottom_row, upper_row, offsets_now, anchor, columns):
    breadth = bottom_row.shape[1]
    device_row = lax.axis_index("gy")
    row_count = lax.axis_size("gy")
    below_shift = offsets_now[device_row]
    above_shift = offsets_now[(device_row + 1) % row_count]
    local_columns = jnp.arange(columns, dtype=jnp.int32)
    down_index = (anchor + below_shift + local_columns) % breadth
    up_index = (anchor - above_shift + local_columns) % breadth
    down_window = jnp.take(bottom_row, down_index, axis=1)
    up_window = jnp.take(upper_row, up_index, axis=1)
    stacked = jnp.stack([down_window, up_window], axis=1)
    rims = padded(stacked, (("gy", 1),), 1)
    return (rims[:, 0, :], rims[:, 3, :])


def block_stencil(field, below_row, above_row, across, coupling):
    diagonal = 1.0 + 4.0 * coupling + 2.0 * VERTICAL
    column_pad = jnp.concatenate([below_row[:, None, :], field, above_row[:, None, :]], axis=1)
    beside = column_pad[:, 2:, :] + column_pad[:, :-2, :] + across
    vertical_sum = jnp.roll(field, 1, 0) + jnp.roll(field, -1, 0)
    return diagonal * field - coupling * beside - VERTICAL * vertical_sum


def block_operate(field, offsets_now, coupling):
    columns = field.shape[2]
    margins = padded(field, (("gx", 2),), 1)
    bottom_full, upper_full = (
        lax.all_gather(field[:, 0, :], "gx", axis=1, tiled=True),
        lax.all_gather(field[:, -1, :], "gx", axis=1, tiled=True),
    )
    right_field = margins[:, :, 2:]
    left_field = margins[:, :, :-2]
    below_row, above_row = sheared(
        bottom_full, upper_full, offsets_now, lax.axis_index("gx") * columns, columns
    )
    across = right_field + left_field
    return (block_stencil(field, below_row, above_row, across, coupling), right_field, left_field)


def block_operate_strip(field, offsets_now, coupling):
    below_row, above_row = sheared(field[:, 0, :], field[:, -1, :], offsets_now, 0, field.shape[2])
    across = jnp.roll(field, 1, 2) + jnp.roll(field, -1, 2)
    return block_stencil(field, below_row, above_row, across, coupling)


def block_coarsest(residual, offsets_now, coupling):
    diagonal = 1.0 + 4.0 * coupling + 2.0 * VERTICAL
    columns = residual.shape[2]
    gathered = lax.all_gather(residual, "gx", axis=2, tiled=True)
    estimate = RELAXATION * gathered / diagonal
    for sweep_index in range(COARSE - 1):
        estimate = (
            estimate
            + RELAXATION * (gathered - block_operate_strip(estimate, offsets_now, coupling)) / diagonal
        )
    return lax.dynamic_slice_in_dim(estimate, lax.axis_index("gx") * columns, columns, 2)


def block_vcycle(residual, offsets_raw, layer_index):
    factor = 2**layer_index
    coupling = DIFFUSION / 4.0**layer_index
    diagonal = 1.0 + 4.0 * coupling + 2.0 * VERTICAL
    offsets_now = offsets_raw // factor
    if layer_index == LEVELS - 1:
        return block_coarsest(residual, offsets_now, coupling)
    estimate = RELAXATION * residual / diagonal
    defect = residual - block_operate(estimate, offsets_now, coupling)[0]
    planes, height, breadth = defect.shape
    coarser = defect.reshape(planes, height // 2, 2, breadth // 2, 2).mean(axis=(2, 4))
    correction = block_vcycle(coarser, offsets_raw, layer_index + 1)
    estimate = estimate + jnp.repeat(jnp.repeat(correction, 2, axis=1), 2, axis=2)
    estimate = (
        estimate + RELAXATION * (residual - block_operate(estimate, offsets_now, coupling)[0]) / diagonal
    )
    return estimate


def total_inner(first_field, second_field):
    return lax.psum(jnp.sum(first_field * second_field), ("gy", "gx"))


def spread(phase, velocity, offsets):
    phase_now = phase
    for time_step in range(STEPS):
        offsets_raw = offsets[time_step]
        applied, right_field, left_field = block_operate(phase_now, offsets_raw, DIFFUSION)
        source = (
            phase_now
            + REACTION * (phase_now - phase_now * phase_now * phase_now)
            - ADVECTION * velocity * (right_field - left_field)
        )
        residual = source - applied
        precond = block_vcycle(residual, offsets_raw, 0)
        projected = total_inner(residual, precond)
        direction = precond
        for iteration in range(ITERS):
            image = block_operate(direction, offsets_raw, DIFFUSION)[0]
            step_size = projected / total_inner(direction, image)
            phase_now = phase_now + step_size * direction
            residual = residual - step_size * image
            if iteration + 1 < ITERS:
                precond = block_vcycle(residual, offsets_raw, 0)
                following = total_inner(residual, precond)
                direction = precond + following / projected * direction
                projected = following
    return phase_now


MOST_DEVICES = 32
MOST_BYTES = 44 << 20


def local(phase, velocity, offsets):
    strips, width = lax.axis_size("gy"), lax.axis_size("gx")
    planes, rows, columns = phase.shape
    sizes = Level(0, width, rows, strips, planes).shape()
    fits = 10 * 4 * sizes[0] * sizes[1] < MOST_BYTES and strips * width <= MOST_DEVICES
    shaped = columns == LANES and rows % 32 == 0 and width in (8, 16, 32, 64) and strips == 4
    if fits and shaped:
        return on_whole(*gathered(phase, velocity), offsets, strips, width)
    return spread(phase, velocity, offsets)


def solution(mesh):
    placed = (P(None, "gy", "gx"), P(None, "gy", "gx"), P())
    return jax.shard_map(local, mesh=mesh, in_specs=placed, out_specs=P(None, "gy", "gx"), check_vma=False)
```

```python
import jax
import jax.numpy as jnp
from jax import lax
from jax.experimental import pallas as pl
from jax.experimental.pallas import tpu as pltpu
from jax.sharding import PartitionSpec as P

STEPS = 2
ITERS = 2
LEVELS = 3
COARSE = 4

RELAXATION = 0.8
DIFFUSION = 4.0
VERTICAL = 1.0
REACTION = 0.5
ADVECTION = 0.5

LANES = 128
SUB = 8


class Level:
    def __init__(self, index, pages, strip_rows, strips, planes):
        self.pages = pages >> index
        self.rows = strip_rows >> index
        self.strips = strips
        self.planes = planes
        self.pitch = self.rows + SUB
        self.height = strips * self.pitch + SUB
        self.factor = 2**index
        self.coupling = DIFFUSION / 4.0**index
        self.diagonal = 1.0 + 4.0 * self.coupling + 2.0 * VERTICAL
        self.relax = RELAXATION / self.diagonal
        self.tiles = self.rows // SUB
        self.count = self.pages * planes

    def shape(self):
        return ((self.count + 2 * self.planes) * self.height, LANES)

    def base(self, strip, tile):
        row = SUB + strip * self.pitch + tile * SUB
        return row if isinstance(row, int) else pl.multiple_of(row, SUB)

    def at(self, page, plane, row):
        return ((page + 1) * self.planes + plane) * self.height + row


def tile_of(ref, level, page, plane, row):
    return ref[pl.ds(level.at(page, plane, row), SUB), :]


def put_tile(ref, level, page, plane, row, value):
    ref[pl.ds(level.at(page, plane, row), SUB), :] = value


def fill_halo(ref, level, offsets, step, halo):
    count, width = level.count, level.pages
    for strip in range(level.strips):
        for tile in range(level.tiles):
            for z in range(level.planes):
                row = level.base(strip, tile)
                put_tile(ref, level, width, z, row, pltpu.roll(tile_of(ref, level, 0, z, row), LANES - 1, 1))
                put_tile(ref, level, -1, z, row, pltpu.roll(tile_of(ref, level, width - 1, z, row), 1, 1))
    for strip in range(level.strips):
        shift = offsets[step, strip] // level.factor
        lane, page = shift // width, shift % width
        under = (strip - 1) % level.strips
        first = level.at(0, 0, SUB + strip * level.pitch)
        last = level.at(0, 0, SUB) + under * level.pitch + level.rows - 1
        upper = ref[pl.ds(first, count, stride=level.height), :]
        lower = ref[pl.ds(last, count, stride=level.height), :]
        start = strip * 4 * count
        halo[pl.ds(start, count), :] = pltpu.roll(upper, (LANES - lane) % LANES, 1)
        halo[pl.ds(start + count, count), :] = pltpu.roll(upper, LANES - 1 - lane, 1)
        halo[pl.ds(start + 2 * count, count), :] = pltpu.roll(lower, (lane + 1) % LANES, 1)
        halo[pl.ds(start + 3 * count, count), :] = pltpu.roll(lower, lane, 1)
        ref[pl.ds(last + 1, count, stride=level.height), :] = halo[pl.ds(start + page * level.planes, count), :]
        ref[pl.ds(first - 1, count, stride=level.height), :] = halo[
            pl.ds(start + 2 * count + (width - page) * level.planes, count), :
        ]


UNROLLED = 16


def repeat(count, body, carry):
    if count > UNROLLED:
        return lax.fori_loop(0, count, body, carry)
    for index in range(count):
        carry = body(index, carry)
    return carry


def stencil(ref, level, base):
    planes, width = level.planes, level.pages
    cell = [[tile_of(ref, level, p, z, base) for z in range(planes)] for p in range(-1, width + 1)]
    out = []
    for p in range(width):
        row = []
        for z in range(planes):
            left, here, right = cell[p][z], cell[p + 1][z], cell[p + 2][z]
            above = tile_of(ref, level, p, z, base + 1)
            below = tile_of(ref, level, p, z, base - 1)
            beside = (above + below) + (right + left)
            vertical = cell[p + 1][(z + 1) % planes] + cell[p + 1][(z - 1) % planes]
            row.append((here, right, left, beside, vertical))
        out.append(row)
    return out


def smooth(level, cell, beside, vertical):
    k = level.relax
    return (1.0 - k * level.diagonal) * cell + (k * level.coupling) * beside + (k * VERTICAL) * vertical


def apply(level, cell, beside, vertical):
    return level.diagonal * cell - level.coupling * beside - VERTICAL * vertical


def loop_coarse(coarse, body):
    count = coarse.strips * coarse.tiles
    if count <= 16:
        for index in range(count):
            body(index, 0)
    else:
        lax.fori_loop(0, count, body, 0)


def restrict(ref, level, coarse_ref, coarse, pairs):
    planes = level.planes

    def body(index, carry):
        strip, tile = index // coarse.tiles, index % coarse.tiles
        room = index * coarse.count * 2 * SUB if isinstance(index, int) else 0
        for half in range(2):
            base = level.base(strip, 2 * tile + half)
            terms = stencil(ref, level, base)
            for p in range(coarse.pages):
                for z in range(planes):
                    total = 0.0
                    for q in (2 * p, 2 * p + 1):
                        cell, _, _, beside, vertical = terms[q][z]
                        total = total + smooth(level, cell, beside, vertical)
                    pairs[pl.ds(room + (p * planes + z) * 2 * SUB + half * SUB, SUB), :] = total
        for p in range(coarse.pages):
            for z in range(planes):
                start = room + (p * planes + z) * 2 * SUB
                even = pairs[pl.ds(start, SUB, stride=2), :]
                odd = pairs[pl.ds(start + 1, SUB, stride=2), :]
                put_tile(coarse_ref, coarse, p, z, coarse.base(strip, tile), 0.25 * (even + odd))
        return carry

    loop_coarse(coarse, body)


def prolong(coarse_ref, coarse, residual, level, ref, pairs):
    planes = level.planes

    def body(index, carry):
        strip, tile = index // coarse.tiles, index % coarse.tiles
        room = index * coarse.count * 2 * SUB if isinstance(index, int) else 0
        for p in range(coarse.pages):
            for z in range(planes):
                start = room + (p * planes + z) * 2 * SUB
                value = tile_of(coarse_ref, coarse, p, z, coarse.base(strip, tile))
                pairs[pl.ds(start, SUB, stride=2), :] = value
                pairs[pl.ds(start + 1, SUB, stride=2), :] = value
        for p in range(coarse.pages):
            for z in range(planes):
                start = room + (p * planes + z) * 2 * SUB
                for half in range(2):
                    value = pairs[pl.ds(start + half * SUB, SUB), :]
                    base = level.base(strip, 2 * tile + half)
                    for q in (2 * p, 2 * p + 1):
                        put_tile(ref, level, q, z, base, level.relax * tile_of(residual, level, q, z, base) + value)
        return carry

    loop_coarse(coarse, body)


def per_tile(level, body, sums):
    def step(index, carry):
        return body(level.base(index // level.tiles, index % level.tiles), carry)

    zero = jnp.zeros((SUB, LANES), jnp.float32)
    return repeat(level.strips * level.tiles, step, (zero,) * sums)


def total(vector):
    return jnp.sum(jnp.sum(vector, axis=0, keepdims=True), axis=1, keepdims=True)


def relaxed(ref, residual, level, target):
    def body(base, carry):
        for p, row in enumerate(stencil(ref, level, base)):
            for z, (cell, _, _, beside, vertical) in enumerate(row):
                value = smooth(level, cell, beside, vertical) + level.relax * tile_of(residual, level, p, z, base)
                put_tile(target, level, p, z, base, value)
        return carry

    per_tile(level, body, 0)


def coarsest(residual, level, offsets, step, spare, halo):
    def first(base, carry):
        for p, row in enumerate(stencil(residual, level, base)):
            for z, (cell, _, _, beside, vertical) in enumerate(row):
                put_tile(spare[0], level, p, z, base, level.relax * (cell + smooth(level, cell, beside, vertical)))
        return carry

    fill_halo(residual, level, offsets, step, halo)
    per_tile(level, first, 0)
    now = 0
    for _ in range(COARSE - 2):
        fill_halo(spare[now], level, offsets, step, halo)
        relaxed(spare[now], residual, level, spare[1 - now])
        now = 1 - now
    return spare[now]


def vcycle(residual, levels, index, offsets, step, work, halo, pairs):
    level, coarse = levels[index], levels[index + 1]
    below, estimate = work[index + 1], work[index][1]
    fill_halo(residual, level, offsets, step, halo)
    restrict(residual, level, below[0], coarse, pairs)
    if index + 2 == LEVELS:
        correction = coarsest(below[0], coarse, offsets, step, below[1:], halo)
    else:
        vcycle(below[0], levels, index + 1, offsets, step, work, halo, pairs)
        correction = below[2]
        relaxed(below[1], below[0], coarse, correction)
    prolong(correction, coarse, residual, level, estimate, pairs)
    fill_halo(estimate, level, offsets, step, halo)


def swap_pages(pages, chosen):
    bit = 1
    while bit < len(pages):
        mask = chosen(bit)
        for p in range(len(pages)):
            if not p & bit:
                a, b = pages[p], pages[p | bit]
                pages[p], pages[p | bit] = jnp.where(mask, b, a), jnp.where(mask, a, b)
        bit *= 2
    return pages


def interleave(block, strips, level, gy, gx, targets, stage):
    width, planes = level.pages, level.planes
    lane = lax.broadcasted_iota(jnp.int32, (SUB, LANES), 1)
    per = LANES // width
    groups = [
        (name, dy, z, tile) for name in range(len(targets)) for dy in range(strips) for z in range(planes) for tile in range(level.tiles)
    ]
    sources = [lane % per * width + jnp.bitwise_xor(lane // per, jnp.bitwise_xor(gx, s)) for s in range(width)]
    for group, (name, dy, z, tile) in enumerate(groups):
        pages = [block(name, dy, p, z, tile) for p in range(width)]
        pages = swap_pages(pages, lambda bit: lane // bit % 2 == 1)
        for p in range(width):
            moved = jnp.take_along_axis(pages[p], sources[p], axis=1)
            stage[pl.ds((group * width + p) * SUB, SUB), :] = moved
    for group, (name, dy, z, tile) in enumerate(groups):
        row = level.base(jnp.bitwise_xor(gy, dy), tile)
        pages = [stage[pl.ds((group * width + p) * SUB, SUB), :] for p in range(width)]
        pages = swap_pages(pages, lambda bit: lane // (per * bit) % 2 == 1)
        for p in range(width):
            put_tile(targets[name], level, jnp.bitwise_xor(gx, p), z, row, pages[p])


def solve(offsets, u, v, r, q, w, work, halo, pairs, levels):
    fine = levels[0]
    e = work[0][1]
    update = None
    for step in range(STEPS):
        fill_halo(u, fine, offsets, step, halo)

        def residual(base, carry):
            for p, row in enumerate(stencil(u, fine, base)):
                for z, (cell, right, left, beside, vertical) in enumerate(row):
                    speed = tile_of(v, fine, p, z, base)
                    cube = cell * cell * cell
                    value = (
                        (1.0 + REACTION - fine.diagonal) * cell
                        - REACTION * cube
                        - ADVECTION * speed * (right - left)
                        + fine.coupling * beside
                        + VERTICAL * vertical
                    )
                    put_tile(r, fine, p, z, base, value)
            return carry

        per_tile(fine, residual, 0)
        vcycle(r, levels, 0, offsets, step, work, halo, pairs)

        def finish(base, carry):
            (rw,) = carry
            for p, row in enumerate(stencil(e, fine, base)):
                for z, (cell, _, _, beside, vertical) in enumerate(row):
                    res = tile_of(r, fine, p, z, base)
                    value = smooth(fine, cell, beside, vertical) + fine.relax * res
                    put_tile(w, fine, p, z, base, value)
                    rw = rw + res * value
            return (rw,)

        (rw,) = per_tile(fine, finish, 1)
        rw = total(rw)
        fill_halo(w, fine, offsets, step, halo)

        def image(base, carry):
            (wq,) = carry
            for p, row in enumerate(stencil(w, fine, base)):
                for z, (cell, _, _, beside, vertical) in enumerate(row):
                    value = apply(fine, cell, beside, vertical)
                    put_tile(q, fine, p, z, base, value)
                    wq = wq + cell * value
            return (wq,)

        (wq,) = per_tile(fine, image, 1)
        alpha = rw / total(wq)
        vcycle(q, levels, 0, offsets, step, work, halo, pairs)

        def finish_next(base, carry):
            (rw,) = carry
            for p, row in enumerate(stencil(e, fine, base)):
                for z, (cell, _, _, beside, vertical) in enumerate(row):
                    img = tile_of(q, fine, p, z, base)
                    value = smooth(fine, cell, beside, vertical) + fine.relax * img
                    res = tile_of(r, fine, p, z, base) - alpha * img
                    value = tile_of(w, fine, p, z, base) - alpha * value
                    put_tile(r, fine, p, z, base, value)
                    rw = rw + res * value
            return (rw,)

        (following,) = per_tile(fine, finish_next, 1)
        following = total(following)
        beta = following / rw
        fill_halo(r, fine, offsets, step, halo)

        def image_next(base, carry):
            (pq,) = carry
            for p, row in enumerate(stencil(r, fine, base)):
                for z, (cell, _, _, beside, vertical) in enumerate(row):
                    direction = cell + beta * tile_of(w, fine, p, z, base)
                    value = apply(fine, cell, beside, vertical) + beta * tile_of(q, fine, p, z, base)
                    pq = pq + direction * value
            return (pq,)

        (pq,) = per_tile(fine, image_next, 1)
        alpha_next = following / total(pq)
        along = alpha + alpha_next * beta

        def update(base, carry):
            for p in range(fine.pages):
                for z in range(fine.planes):
                    value = (
                        tile_of(u, fine, p, z, base)
                        + along * tile_of(w, fine, p, z, base)
                        + alpha_next * tile_of(r, fine, p, z, base)
                    )
                    put_tile(u, fine, p, z, base, value)
            return carry

        if step + 1 < STEPS:
            per_tile(fine, update, 0)
    return update


def whole_kernel(places, arrays, levels, *refs):
    offsets, held, out = refs[0], refs[1 : 1 + arrays], refs[1 + arrays]
    u, v, r, q, w, e, r1, e1, f1, r2, e2, f2, halo, pairs, stage = refs[2 + arrays :]
    fine = levels[0]
    gy, gx = lax.axis_index("gy"), lax.axis_index("gx")

    def block(name, dy, dx, z, tile):
        array, place = places[name, dy, dx]
        return held[array][(*place, z, pl.ds(tile * SUB, SUB), slice(None))]

    interleave(block, fine.strips, fine, gy, gx, (u, v), stage)
    work = [[r, e], [r1, e1, f1], [r2, e2, f2]]
    update = solve(offsets, u, v, r, q, w, work, halo, pairs, levels)
    lane = lax.broadcasted_iota(jnp.int32, (SUB, LANES), 1)
    source = gx * (LANES // fine.pages) + lane // fine.pages
    for tile in range(fine.tiles):
        base = fine.base(gy, tile)
        update(base, ())
        for z in range(fine.planes):
            value = jnp.zeros((SUB, LANES), jnp.float32)
            for p in range(fine.pages):
                page = jnp.take_along_axis(tile_of(u, fine, p, z, base), source, axis=1)
                value = jnp.where(lane % fine.pages == p, page, value)
            out[z, pl.ds(tile * SUB, SUB), :] = value


def on_whole(arrays, places, offsets, strips, width):
    planes, rows, columns = arrays[0].shape[-3:]
    levels = [Level(i, width, rows, strips, planes) for i in range(LEVELS)]
    fields = [pltpu.VMEM(levels[0].shape(), jnp.float32)] * 6
    fields += [pltpu.VMEM(levels[1].shape(), jnp.float32)] * 3 + [pltpu.VMEM(levels[2].shape(), jnp.float32)] * 3
    count = levels[0].count
    scratch = fields + [
        pltpu.VMEM((strips * 4 * count, LANES), jnp.float32),
        pltpu.VMEM((planes * strips * rows * width // 2, LANES), jnp.float32),
        pltpu.VMEM((2 * planes * strips * rows * width, LANES), jnp.float32),
    ]

    def kernel(*refs):
        whole_kernel(places, len(arrays), levels, *refs)

    return pl.pallas_call(
        kernel,
        out_shape=jax.ShapeDtypeStruct((planes, rows, columns), jnp.float32),
        in_specs=[pl.BlockSpec(memory_space=pltpu.SMEM)] + [pl.BlockSpec(memory_space=pltpu.VMEM)] * len(arrays),
        out_specs=pl.BlockSpec(memory_space=pltpu.VMEM),
        scratch_shapes=scratch,
        compiler_params=pltpu.CompilerParams(vmem_limit_bytes=48 << 20),
    )(offsets, *arrays)


def swapped(block, axis, bits):
    count = lax.axis_size(axis)
    return lax.ppermute(block, axis, [(i, i ^ bits) for i in range(count)])


def gathered(phase, velocity):
    width = lax.axis_size("gx")
    steps = list(range(0, width, 2))
    arrays, places = [], {}
    for name, own in enumerate((phase, velocity)):
        own = own[None]
        got = {k: swapped(own, "gx", k) for k in steps[1:]}
        line = jnp.concatenate([own] + [got[k] for k in steps[1:]])
        across = swapped(line, "gx", 1)
        along = swapped(line, "gy", 2)
        corner = swapped(along, "gx", 1) if name else swapped(across, "gy", 2)
        for dy, dx, array in ((0, 0, line), (0, 1, across), (2, 0, along), (2, 1, corner)):
            for core in range(2):
                for i, k in enumerate(steps):
                    places[name, dy ^ core, dx ^ k] = (len(arrays), (i,))
                arrays.append(swapped(array, "gy", 1) if core else array)
    return arrays, places


def padded(cells, sides, width):
    for axis, dim in sides:
        count = lax.axis_size(axis)
        head = lax.slice_in_dim(cells, 0, width, axis=dim)
        tail = lax.slice_in_dim(cells, cells.shape[dim] - width, cells.shape[dim], axis=dim)
        cells = jnp.concatenate(
            [
                lax.ppermute(tail, axis, [(i, (i + 1) % count) for i in range(count)]),
                cells,
                lax.ppermute(head, axis, [((i + 1) % count, i) for i in range(count)]),
            ],
            axis=dim,
        )
    return cells


def sheared(bottom_row, upper_row, offsets_now, anchor, columns):
    breadth = bottom_row.shape[1]
    device_row = lax.axis_index("gy")
    row_count = lax.axis_size("gy")
    below_shift = offsets_now[device_row]
    above_shift = offsets_now[(device_row + 1) % row_count]
    local_columns = jnp.arange(columns, dtype=jnp.int32)
    down_index = (anchor + below_shift + local_columns) % breadth
    up_index = (anchor - above_shift + local_columns) % breadth
    down_window = jnp.take(bottom_row, down_index, axis=1)
    up_window = jnp.take(upper_row, up_index, axis=1)
    stacked = jnp.stack([down_window, up_window], axis=1)
    rims = padded(stacked, (("gy", 1),), 1)
    return (rims[:, 0, :], rims[:, 3, :])


def block_stencil(field, below_row, above_row, across, coupling):
    diagonal = 1.0 + 4.0 * coupling + 2.0 * VERTICAL
    column_pad = jnp.concatenate([below_row[:, None, :], field, above_row[:, None, :]], axis=1)
    beside = column_pad[:, 2:, :] + column_pad[:, :-2, :] + across
    vertical_sum = jnp.roll(field, 1, 0) + jnp.roll(field, -1, 0)
    return diagonal * field - coupling * beside - VERTICAL * vertical_sum


def block_operate(field, offsets_now, coupling):
    columns = field.shape[2]
    margins = padded(field, (("gx", 2),), 1)
    bottom_full, upper_full = (
        lax.all_gather(field[:, 0, :], "gx", axis=1, tiled=True),
        lax.all_gather(field[:, -1, :], "gx", axis=1, tiled=True),
    )
    right_field = margins[:, :, 2:]
    left_field = margins[:, :, :-2]
    below_row, above_row = sheared(
        bottom_full, upper_full, offsets_now, lax.axis_index("gx") * columns, columns
    )
    across = right_field + left_field
    return (block_stencil(field, below_row, above_row, across, coupling), right_field, left_field)


def block_operate_strip(field, offsets_now, coupling):
    below_row, above_row = sheared(field[:, 0, :], field[:, -1, :], offsets_now, 0, field.shape[2])
    across = jnp.roll(field, 1, 2) + jnp.roll(field, -1, 2)
    return block_stencil(field, below_row, above_row, across, coupling)


def block_coarsest(residual, offsets_now, coupling):
    diagonal = 1.0 + 4.0 * coupling + 2.0 * VERTICAL
    columns = residual.shape[2]
    gathered = lax.all_gather(residual, "gx", axis=2, tiled=True)
    estimate = RELAXATION * gathered / diagonal
    for sweep_index in range(COARSE - 1):
        estimate = (
            estimate
            + RELAXATION * (gathered - block_operate_strip(estimate, offsets_now, coupling)) / diagonal
        )
    return lax.dynamic_slice_in_dim(estimate, lax.axis_index("gx") * columns, columns, 2)


def block_vcycle(residual, offsets_raw, layer_index):
    factor = 2**layer_index
    coupling = DIFFUSION / 4.0**layer_index
    diagonal = 1.0 + 4.0 * coupling + 2.0 * VERTICAL
    offsets_now = offsets_raw // factor
    if layer_index == LEVELS - 1:
        return block_coarsest(residual, offsets_now, coupling)
    estimate = RELAXATION * residual / diagonal
    defect = residual - block_operate(estimate, offsets_now, coupling)[0]
    planes, height, breadth = defect.shape
    coarser = defect.reshape(planes, height // 2, 2, breadth // 2, 2).mean(axis=(2, 4))
    correction = block_vcycle(coarser, offsets_raw, layer_index + 1)
    estimate = estimate + jnp.repeat(jnp.repeat(correction, 2, axis=1), 2, axis=2)
    estimate = (
        estimate + RELAXATION * (residual - block_operate(estimate, offsets_now, coupling)[0]) / diagonal
    )
    return estimate


def total_inner(first_field, second_field):
    return lax.psum(jnp.sum(first_field * second_field), ("gy", "gx"))


def spread(phase, velocity, offsets):
    phase_now = phase
    for time_step in range(STEPS):
        offsets_raw = offsets[time_step]
        applied, right_field, left_field = block_operate(phase_now, offsets_raw, DIFFUSION)
        source = (
            phase_now
            + REACTION * (phase_now - phase_now * phase_now * phase_now)
            - ADVECTION * velocity * (right_field - left_field)
        )
        residual = source - applied
        precond = block_vcycle(residual, offsets_raw, 0)
        projected = total_inner(residual, precond)
        direction = precond
        for iteration in range(ITERS):
            image = block_operate(direction, offsets_raw, DIFFUSION)[0]
            step_size = projected / total_inner(direction, image)
            phase_now = phase_now + step_size * direction
            residual = residual - step_size * image
            if iteration + 1 < ITERS:
                precond = block_vcycle(residual, offsets_raw, 0)
                following = total_inner(residual, precond)
                direction = precond + following / projected * direction
                projected = following
    return phase_now


MOST_DEVICES = 32
MOST_BYTES = 44 << 20


def local(phase, velocity, offsets):
    strips, width = lax.axis_size("gy"), lax.axis_size("gx")
    planes, rows, columns = phase.shape
    sizes = Level(0, width, rows, strips, planes).shape()
    fits = 10 * 4 * sizes[0] * sizes[1] < MOST_BYTES and strips * width <= MOST_DEVICES
    shaped = columns == LANES and rows % 32 == 0 and width in (8, 16, 32, 64) and strips == 4
    if fits and shaped:
        return on_whole(*gathered(phase, velocity), offsets, strips, width)
    return spread(phase, velocity, offsets)


def solution(mesh):
    placed = (P(None, "gy", "gx"), P(None, "gy", "gx"), P())
    return jax.shard_map(local, mesh=mesh, in_specs=placed, out_specs=P(None, "gy", "gx"), check_vma=False)
```

```python
import jax
import jax.numpy as jnp
from jax import lax
from jax.experimental import pallas as pl
from jax.experimental.pallas import tpu as pltpu
from jax.sharding import PartitionSpec as P

STEPS = 2
ITERS = 2
LEVELS = 3
COARSE = 4

RELAXATION = 0.8
DIFFUSION = 4.0
VERTICAL = 1.0
REACTION = 0.5
ADVECTION = 0.5

LANES = 128
SUB = 8


class Level:
    def __init__(self, index, pages, strip_rows, strips, planes):
        self.pages = pages >> index
        self.rows = strip_rows >> index
        self.strips = strips
        self.planes = planes
        self.pitch = self.rows + SUB
        self.height = strips * self.pitch + SUB
        self.factor = 2**index
        self.coupling = DIFFUSION / 4.0**index
        self.diagonal = 1.0 + 4.0 * self.coupling + 2.0 * VERTICAL
        self.relax = RELAXATION / self.diagonal
        self.tiles = self.rows // SUB
        self.count = self.pages * planes

    def shape(self):
        return ((self.count + 2 * self.planes) * self.height, LANES)

    def base(self, strip, tile):
        row = SUB + strip * self.pitch + tile * SUB
        return row if isinstance(row, int) else pl.multiple_of(row, SUB)

    def at(self, page, plane, row):
        return ((page + 1) * self.planes + plane) * self.height + row


def tile_of(ref, level, page, plane, row):
    return ref[pl.ds(level.at(page, plane, row), SUB), :]


def put_tile(ref, level, page, plane, row, value):
    ref[pl.ds(level.at(page, plane, row), SUB), :] = value


def fill_halo(ref, level, offsets, step, halo):
    count, width = level.count, level.pages
    for strip in range(level.strips):
        for tile in range(level.tiles):
            for z in range(level.planes):
                row = level.base(strip, tile)
                put_tile(ref, level, width, z, row, pltpu.roll(tile_of(ref, level, 0, z, row), LANES - 1, 1))
                put_tile(ref, level, -1, z, row, pltpu.roll(tile_of(ref, level, width - 1, z, row), 1, 1))
    for strip in range(level.strips):
        shift = offsets[step, strip] // level.factor
        lane, page = shift // width, shift % width
        under = (strip - 1) % level.strips
        first = level.at(0, 0, SUB + strip * level.pitch)
        last = level.at(0, 0, SUB) + under * level.pitch + level.rows - 1
        upper = ref[pl.ds(first, count, stride=level.height), :]
        lower = ref[pl.ds(last, count, stride=level.height), :]
        start = strip * 4 * count
        halo[pl.ds(start, count), :] = pltpu.roll(upper, (LANES - lane) % LANES, 1)
        halo[pl.ds(start + count, count), :] = pltpu.roll(upper, LANES - 1 - lane, 1)
        halo[pl.ds(start + 2 * count, count), :] = pltpu.roll(lower, (lane + 1) % LANES, 1)
        halo[pl.ds(start + 3 * count, count), :] = pltpu.roll(lower, lane, 1)
        ref[pl.ds(last + 1, count, stride=level.height), :] = halo[pl.ds(start + page * level.planes, count), :]
        ref[pl.ds(first - 1, count, stride=level.height), :] = halo[
            pl.ds(start + 2 * count + (width - page) * level.planes, count), :
        ]


UNROLLED = 16


def repeat(count, body, carry):
    if count > UNROLLED:
        return lax.fori_loop(0, count, body, carry)
    for index in range(count):
        carry = body(index, carry)
    return carry


def stencil(ref, level, base):
    planes, width = level.planes, level.pages
    cell = [[tile_of(ref, level, p, z, base) for z in range(planes)] for p in range(-1, width + 1)]
    out = []
    for p in range(width):
        row = []
        for z in range(planes):
            left, here, right = cell[p][z], cell[p + 1][z], cell[p + 2][z]
            above = tile_of(ref, level, p, z, base + 1)
            below = tile_of(ref, level, p, z, base - 1)
            beside = (above + below) + (right + left)
            vertical = cell[p + 1][(z + 1) % planes] + cell[p + 1][(z - 1) % planes]
            row.append((here, right, left, beside, vertical))
        out.append(row)
    return out


def smooth(level, cell, beside, vertical):
    k = level.relax
    return (1.0 - k * level.diagonal) * cell + (k * level.coupling) * beside + (k * VERTICAL) * vertical


def apply(level, cell, beside, vertical):
    return level.diagonal * cell - level.coupling * beside - VERTICAL * vertical


def loop_coarse(coarse, body):
    count = coarse.strips * coarse.tiles
    if count <= 16:
        for index in range(count):
            body(index, 0)
    else:
        lax.fori_loop(0, count, body, 0)


def restrict(ref, level, coarse_ref, coarse, pairs):
    planes = level.planes

    def body(index, carry):
        strip, tile = index // coarse.tiles, index % coarse.tiles
        room = index * coarse.count * 2 * SUB if isinstance(index, int) else 0
        for half in range(2):
            base = level.base(strip, 2 * tile + half)
            terms = stencil(ref, level, base)
            for p in range(coarse.pages):
                for z in range(planes):
                    total = 0.0
                    for q in (2 * p, 2 * p + 1):
                        cell, _, _, beside, vertical = terms[q][z]
                        total = total + smooth(level, cell, beside, vertical)
                    pairs[pl.ds(room + (p * planes + z) * 2 * SUB + half * SUB, SUB), :] = total
        for p in range(coarse.pages):
            for z in range(planes):
                start = room + (p * planes + z) * 2 * SUB
                even = pairs[pl.ds(start, SUB, stride=2), :]
                odd = pairs[pl.ds(start + 1, SUB, stride=2), :]
                put_tile(coarse_ref, coarse, p, z, coarse.base(strip, tile), 0.25 * (even + odd))
        return carry

    loop_coarse(coarse, body)


def prolong(coarse_ref, coarse, residual, level, ref, pairs):
    planes = level.planes

    def body(index, carry):
        strip, tile = index // coarse.tiles, index % coarse.tiles
        room = index * coarse.count * 2 * SUB if isinstance(index, int) else 0
        for p in range(coarse.pages):
            for z in range(planes):
                start = room + (p * planes + z) * 2 * SUB
                value = tile_of(coarse_ref, coarse, p, z, coarse.base(strip, tile))
                pairs[pl.ds(start, SUB, stride=2), :] = value
                pairs[pl.ds(start + 1, SUB, stride=2), :] = value
        for p in range(coarse.pages):
            for z in range(planes):
                start = room + (p * planes + z) * 2 * SUB
                for half in range(2):
                    value = pairs[pl.ds(start + half * SUB, SUB), :]
                    base = level.base(strip, 2 * tile + half)
                    for q in (2 * p, 2 * p + 1):
                        put_tile(ref, level, q, z, base, level.relax * tile_of(residual, level, q, z, base) + value)
        return carry

    loop_coarse(coarse, body)


def per_tile(level, body, sums):
    def step(index, carry):
        return body(level.base(index // level.tiles, index % level.tiles), carry)

    zero = jnp.zeros((SUB, LANES), jnp.float32)
    return repeat(level.strips * level.tiles, step, (zero,) * sums)


def total(vector):
    return jnp.sum(jnp.sum(vector, axis=0, keepdims=True), axis=1, keepdims=True)


def relaxed(ref, residual, level, target):
    def body(base, carry):
        for p, row in enumerate(stencil(ref, level, base)):
            for z, (cell, _, _, beside, vertical) in enumerate(row):
                value = smooth(level, cell, beside, vertical) + level.relax * tile_of(residual, level, p, z, base)
                put_tile(target, level, p, z, base, value)
        return carry

    per_tile(level, body, 0)


def coarsest(residual, level, offsets, step, spare, halo):
    def first(base, carry):
        for p, row in enumerate(stencil(residual, level, base)):
            for z, (cell, _, _, beside, vertical) in enumerate(row):
                put_tile(spare[0], level, p, z, base, level.relax * (cell + smooth(level, cell, beside, vertical)))
        return carry

    fill_halo(residual, level, offsets, step, halo)
    per_tile(level, first, 0)
    now = 0
    for _ in range(COARSE - 2):
        fill_halo(spare[now], level, offsets, step, halo)
        relaxed(spare[now], residual, level, spare[1 - now])
        now = 1 - now
    return spare[now]


def vcycle(residual, levels, index, offsets, step, work, halo, pairs):
    level, coarse = levels[index], levels[index + 1]
    below, estimate = work[index + 1], work[index][1]
    fill_halo(residual, level, offsets, step, halo)
    restrict(residual, level, below[0], coarse, pairs)
    if index + 2 == LEVELS:
        correction = coarsest(below[0], coarse, offsets, step, below[1:], halo)
    else:
        vcycle(below[0], levels, index + 1, offsets, step, work, halo, pairs)
        correction = below[2]
        relaxed(below[1], below[0], coarse, correction)
    prolong(correction, coarse, residual, level, estimate, pairs)
    fill_halo(estimate, level, offsets, step, halo)


def swap_pages(pages, chosen):
    bit = 1
    while bit < len(pages):
        mask = chosen(bit)
        for p in range(len(pages)):
            if not p & bit:
                a, b = pages[p], pages[p | bit]
                pages[p], pages[p | bit] = jnp.where(mask, b, a), jnp.where(mask, a, b)
        bit *= 2
    return pages


def interleave(block, strips, level, gy, gx, targets, stage):
    width, planes = level.pages, level.planes
    lane = lax.broadcasted_iota(jnp.int32, (SUB, LANES), 1)
    per = LANES // width
    groups = [
        (name, dy, z, tile) for name in range(len(targets)) for dy in range(strips) for z in range(planes) for tile in range(level.tiles)
    ]
    sources = [lane % per * width + jnp.bitwise_xor(lane // per, jnp.bitwise_xor(gx, s)) for s in range(width)]
    for group, (name, dy, z, tile) in enumerate(groups):
        pages = [block(name, dy, p, z, tile) for p in range(width)]
        pages = swap_pages(pages, lambda bit: lane // bit % 2 == 1)
        for p in range(width):
            moved = jnp.take_along_axis(pages[p], sources[p], axis=1)
            stage[pl.ds((group * width + p) * SUB, SUB), :] = moved
    for group, (name, dy, z, tile) in enumerate(groups):
        row = level.base(jnp.bitwise_xor(gy, dy), tile)
        pages = [stage[pl.ds((group * width + p) * SUB, SUB), :] for p in range(width)]
        pages = swap_pages(pages, lambda bit: lane // (per * bit) % 2 == 1)
        for p in range(width):
            put_tile(targets[name], level, jnp.bitwise_xor(gx, p), z, row, pages[p])


def solve(offsets, u, v, r, q, w, work, halo, pairs, levels):
    fine = levels[0]
    e = work[0][1]
    update = None
    for step in range(STEPS):
        fill_halo(u, fine, offsets, step, halo)

        def residual(base, carry):
            for p, row in enumerate(stencil(u, fine, base)):
                for z, (cell, right, left, beside, vertical) in enumerate(row):
                    speed = tile_of(v, fine, p, z, base)
                    cube = cell * cell * cell
                    value = (
                        (1.0 + REACTION - fine.diagonal) * cell
                        - REACTION * cube
                        - ADVECTION * speed * (right - left)
                        + fine.coupling * beside
                        + VERTICAL * vertical
                    )
                    put_tile(r, fine, p, z, base, value)
            return carry

        per_tile(fine, residual, 0)
        vcycle(r, levels, 0, offsets, step, work, halo, pairs)

        def finish(base, carry):
            (rw,) = carry
            for p, row in enumerate(stencil(e, fine, base)):
                for z, (cell, _, _, beside, vertical) in enumerate(row):
                    res = tile_of(r, fine, p, z, base)
                    value = smooth(fine, cell, beside, vertical) + fine.relax * res
                    put_tile(w, fine, p, z, base, value)
                    rw = rw + res * value
            return (rw,)

        (rw,) = per_tile(fine, finish, 1)
        rw = total(rw)
        fill_halo(w, fine, offsets, step, halo)

        def image(base, carry):
            (wq,) = carry
            for p, row in enumerate(stencil(w, fine, base)):
                for z, (cell, _, _, beside, vertical) in enumerate(row):
                    value = apply(fine, cell, beside, vertical)
                    put_tile(q, fine, p, z, base, value)
                    wq = wq + cell * value
            return (wq,)

        (wq,) = per_tile(fine, image, 1)
        alpha = rw / total(wq)
        vcycle(q, levels, 0, offsets, step, work, halo, pairs)

        def finish_next(base, carry):
            (rw,) = carry
            for p, row in enumerate(stencil(e, fine, base)):
                for z, (cell, _, _, beside, vertical) in enumerate(row):
                    img = tile_of(q, fine, p, z, base)
                    value = smooth(fine, cell, beside, vertical) + fine.relax * img
                    res = tile_of(r, fine, p, z, base) - alpha * img
                    value = tile_of(w, fine, p, z, base) - alpha * value
                    put_tile(r, fine, p, z, base, value)
                    rw = rw + res * value
            return (rw,)

        (following,) = per_tile(fine, finish_next, 1)
        following = total(following)
        beta = following / rw
        fill_halo(r, fine, offsets, step, halo)

        def image_next(base, carry):
            (pq,) = carry
            for p, row in enumerate(stencil(r, fine, base)):
                for z, (cell, _, _, beside, vertical) in enumerate(row):
                    direction = cell + beta * tile_of(w, fine, p, z, base)
                    value = apply(fine, cell, beside, vertical) + beta * tile_of(q, fine, p, z, base)
                    pq = pq + direction * value
            return (pq,)

        (pq,) = per_tile(fine, image_next, 1)
        alpha_next = following / total(pq)
        along = alpha + alpha_next * beta

        def update(base, carry):
            for p in range(fine.pages):
                for z in range(fine.planes):
                    value = (
                        tile_of(u, fine, p, z, base)
                        + along * tile_of(w, fine, p, z, base)
                        + alpha_next * tile_of(r, fine, p, z, base)
                    )
                    put_tile(u, fine, p, z, base, value)
            return carry

        if step + 1 < STEPS:
            per_tile(fine, update, 0)
    return update


def whole_kernel(places, arrays, levels, *refs):
    offsets, held, out = refs[0], refs[1 : 1 + arrays], refs[1 + arrays]
    u, v, r, q, w, e, r1, e1, f1, r2, e2, f2, halo, pairs, stage = refs[2 + arrays :]
    fine = levels[0]
    gy, gx = lax.axis_index("gy"), lax.axis_index("gx")

    def block(name, dy, dx, z, tile):
        array, place = places[name, dy, dx]
        return held[array][(*place, z, pl.ds(tile * SUB, SUB), slice(None))]

    interleave(block, fine.strips, fine, gy, gx, (u, v), stage)
    work = [[r, e], [r1, e1, f1], [r2, e2, f2]]
    update = solve(offsets, u, v, r, q, w, work, halo, pairs, levels)
    lane = lax.broadcasted_iota(jnp.int32, (SUB, LANES), 1)
    source = gx * (LANES // fine.pages) + lane // fine.pages
    for tile in range(fine.tiles):
        base = fine.base(gy, tile)
        update(base, ())
        for z in range(fine.planes):
            value = jnp.zeros((SUB, LANES), jnp.float32)
            for p in range(fine.pages):
                page = jnp.take_along_axis(tile_of(u, fine, p, z, base), source, axis=1)
                value = jnp.where(lane % fine.pages == p, page, value)
            out[z, pl.ds(tile * SUB, SUB), :] = value


def on_whole(arrays, places, offsets, strips, width):
    planes, rows, columns = arrays[0].shape[-3:]
    levels = [Level(i, width, rows, strips, planes) for i in range(LEVELS)]
    fields = [pltpu.VMEM(levels[0].shape(), jnp.float32)] * 6
    fields += [pltpu.VMEM(levels[1].shape(), jnp.float32)] * 3 + [pltpu.VMEM(levels[2].shape(), jnp.float32)] * 3
    count = levels[0].count
    scratch = fields + [
        pltpu.VMEM((strips * 4 * count, LANES), jnp.float32),
        pltpu.VMEM((planes * strips * rows * width // 2, LANES), jnp.float32),
        pltpu.VMEM((2 * planes * strips * rows * width, LANES), jnp.float32),
    ]

    def kernel(*refs):
        whole_kernel(places, len(arrays), levels, *refs)

    return pl.pallas_call(
        kernel,
        out_shape=jax.ShapeDtypeStruct((planes, rows, columns), jnp.float32),
        in_specs=[pl.BlockSpec(memory_space=pltpu.SMEM)] + [pl.BlockSpec(memory_space=pltpu.VMEM)] * len(arrays),
        out_specs=pl.BlockSpec(memory_space=pltpu.VMEM),
        scratch_shapes=scratch,
        compiler_params=pltpu.CompilerParams(vmem_limit_bytes=48 << 20),
    )(offsets, *arrays)


def swapped(block, axis, bits):
    count = lax.axis_size(axis)
    return lax.ppermute(block, axis, [(i, i ^ bits) for i in range(count)])


def gathered(phase, velocity):
    width = lax.axis_size("gx")
    steps = list(range(0, width, 2))
    both = jnp.stack([phase, velocity])
    far = swapped(both, "gx", steps[-1])
    arrays, places = [], {}
    for name, own in enumerate((phase, velocity)):
        got = [swapped(own[None], "gx", k) for k in steps[1:-1]]
        line = jnp.concatenate([both[name : name + 1]] + got + [far[name : name + 1]])
        across = swapped(line, "gx", 1)
        along = swapped(line, "gy", 2)
        corner = swapped(along, "gx", 1) if name else swapped(across, "gy", 2)
        for dy, dx, array in ((0, 0, line), (0, 1, across), (2, 0, along), (2, 1, corner)):
            for core in range(2):
                for i, k in enumerate(steps):
                    places[name, dy ^ core, dx ^ k] = (len(arrays), (i,))
                arrays.append(swapped(array, "gy", 1) if core else array)
    return arrays, places


def padded(cells, sides, width):
    for axis, dim in sides:
        count = lax.axis_size(axis)
        head = lax.slice_in_dim(cells, 0, width, axis=dim)
        tail = lax.slice_in_dim(cells, cells.shape[dim] - width, cells.shape[dim], axis=dim)
        cells = jnp.concatenate(
            [
                lax.ppermute(tail, axis, [(i, (i + 1) % count) for i in range(count)]),
                cells,
                lax.ppermute(head, axis, [((i + 1) % count, i) for i in range(count)]),
            ],
            axis=dim,
        )
    return cells


def sheared(bottom_row, upper_row, offsets_now, anchor, columns):
    breadth = bottom_row.shape[1]
    device_row = lax.axis_index("gy")
    row_count = lax.axis_size("gy")
    below_shift = offsets_now[device_row]
    above_shift = offsets_now[(device_row + 1) % row_count]
    local_columns = jnp.arange(columns, dtype=jnp.int32)
    down_index = (anchor + below_shift + local_columns) % breadth
    up_index = (anchor - above_shift + local_columns) % breadth
    down_window = jnp.take(bottom_row, down_index, axis=1)
    up_window = jnp.take(upper_row, up_index, axis=1)
    stacked = jnp.stack([down_window, up_window], axis=1)
    rims = padded(stacked, (("gy", 1),), 1)
    return (rims[:, 0, :], rims[:, 3, :])


def block_stencil(field, below_row, above_row, across, coupling):
    diagonal = 1.0 + 4.0 * coupling + 2.0 * VERTICAL
    column_pad = jnp.concatenate([below_row[:, None, :], field, above_row[:, None, :]], axis=1)
    beside = column_pad[:, 2:, :] + column_pad[:, :-2, :] + across
    vertical_sum = jnp.roll(field, 1, 0) + jnp.roll(field, -1, 0)
    return diagonal * field - coupling * beside - VERTICAL * vertical_sum


def block_operate(field, offsets_now, coupling):
    columns = field.shape[2]
    margins = padded(field, (("gx", 2),), 1)
    bottom_full, upper_full = (
        lax.all_gather(field[:, 0, :], "gx", axis=1, tiled=True),
        lax.all_gather(field[:, -1, :], "gx", axis=1, tiled=True),
    )
    right_field = margins[:, :, 2:]
    left_field = margins[:, :, :-2]
    below_row, above_row = sheared(
        bottom_full, upper_full, offsets_now, lax.axis_index("gx") * columns, columns
    )
    across = right_field + left_field
    return (block_stencil(field, below_row, above_row, across, coupling), right_field, left_field)


def block_operate_strip(field, offsets_now, coupling):
    below_row, above_row = sheared(field[:, 0, :], field[:, -1, :], offsets_now, 0, field.shape[2])
    across = jnp.roll(field, 1, 2) + jnp.roll(field, -1, 2)
    return block_stencil(field, below_row, above_row, across, coupling)


def block_coarsest(residual, offsets_now, coupling):
    diagonal = 1.0 + 4.0 * coupling + 2.0 * VERTICAL
    columns = residual.shape[2]
    gathered = lax.all_gather(residual, "gx", axis=2, tiled=True)
    estimate = RELAXATION * gathered / diagonal
    for sweep_index in range(COARSE - 1):
        estimate = (
            estimate
            + RELAXATION * (gathered - block_operate_strip(estimate, offsets_now, coupling)) / diagonal
        )
    return lax.dynamic_slice_in_dim(estimate, lax.axis_index("gx") * columns, columns, 2)


def block_vcycle(residual, offsets_raw, layer_index):
    factor = 2**layer_index
    coupling = DIFFUSION / 4.0**layer_index
    diagonal = 1.0 + 4.0 * coupling + 2.0 * VERTICAL
    offsets_now = offsets_raw // factor
    if layer_index == LEVELS - 1:
        return block_coarsest(residual, offsets_now, coupling)
    estimate = RELAXATION * residual / diagonal
    defect = residual - block_operate(estimate, offsets_now, coupling)[0]
    planes, height, breadth = defect.shape
    coarser = defect.reshape(planes, height // 2, 2, breadth // 2, 2).mean(axis=(2, 4))
    correction = block_vcycle(coarser, offsets_raw, layer_index + 1)
    estimate = estimate + jnp.repeat(jnp.repeat(correction, 2, axis=1), 2, axis=2)
    estimate = (
        estimate + RELAXATION * (residual - block_operate(estimate, offsets_now, coupling)[0]) / diagonal
    )
    return estimate


def total_inner(first_field, second_field):
    return lax.psum(jnp.sum(first_field * second_field), ("gy", "gx"))


def spread(phase, velocity, offsets):
    phase_now = phase
    for time_step in range(STEPS):
        offsets_raw = offsets[time_step]
        applied, right_field, left_field = block_operate(phase_now, offsets_raw, DIFFUSION)
        source = (
            phase_now
            + REACTION * (phase_now - phase_now * phase_now * phase_now)
            - ADVECTION * velocity * (right_field - left_field)
        )
        residual = source - applied
        precond = block_vcycle(residual, offsets_raw, 0)
        projected = total_inner(residual, precond)
        direction = precond
        for iteration in range(ITERS):
            image = block_operate(direction, offsets_raw, DIFFUSION)[0]
            step_size = projected / total_inner(direction, image)
            phase_now = phase_now + step_size * direction
            residual = residual - step_size * image
            if iteration + 1 < ITERS:
                precond = block_vcycle(residual, offsets_raw, 0)
                following = total_inner(residual, precond)
                direction = precond + following / projected * direction
                projected = following
    return phase_now


MOST_DEVICES = 32
MOST_BYTES = 44 << 20


def local(phase, velocity, offsets):
    strips, width = lax.axis_size("gy"), lax.axis_size("gx")
    planes, rows, columns = phase.shape
    sizes = Level(0, width, rows, strips, planes).shape()
    fits = 10 * 4 * sizes[0] * sizes[1] < MOST_BYTES and strips * width <= MOST_DEVICES
    shaped = columns == LANES and rows % 32 == 0 and width in (8, 16, 32, 64) and strips == 4
    if fits and shaped:
        return on_whole(*gathered(phase, velocity), offsets, strips, width)
    return spread(phase, velocity, offsets)


def solution(mesh):
    placed = (P(None, "gy", "gx"), P(None, "gy", "gx"), P())
    return jax.shard_map(local, mesh=mesh, in_specs=placed, out_specs=P(None, "gy", "gx"), check_vma=False)
```

```python
import jax
import jax.numpy as jnp
from jax import lax
from jax.experimental import pallas as pl
from jax.experimental.pallas import tpu as pltpu
from jax.sharding import PartitionSpec as P

STEPS = 2
ITERS = 2
LEVELS = 3
COARSE = 4

RELAXATION = 0.8
DIFFUSION = 4.0
VERTICAL = 1.0
REACTION = 0.5
ADVECTION = 0.5

LANES = 128
SUB = 8


class Level:
    def __init__(self, index, pages, strip_rows, strips, planes):
        self.pages = pages >> index
        self.rows = strip_rows >> index
        self.strips = strips
        self.planes = planes
        self.pitch = self.rows + SUB
        self.height = strips * self.pitch + SUB
        self.factor = 2**index
        self.coupling = DIFFUSION / 4.0**index
        self.diagonal = 1.0 + 4.0 * self.coupling + 2.0 * VERTICAL
        self.relax = RELAXATION / self.diagonal
        self.tiles = self.rows // SUB
        self.count = self.pages * planes

    def shape(self):
        return ((self.count + 2 * self.planes) * self.height, LANES)

    def base(self, strip, tile):
        row = SUB + strip * self.pitch + tile * SUB
        return row if isinstance(row, int) else pl.multiple_of(row, SUB)

    def at(self, page, plane, row):
        return ((page + 1) * self.planes + plane) * self.height + row


def tile_of(ref, level, page, plane, row):
    return ref[pl.ds(level.at(page, plane, row), SUB), :]


def put_tile(ref, level, page, plane, row, value):
    ref[pl.ds(level.at(page, plane, row), SUB), :] = value


def fill_halo(ref, level, offsets, step, halo):
    count, width = level.count, level.pages
    for strip in range(level.strips):
        for tile in range(level.tiles):
            for z in range(level.planes):
                row = level.base(strip, tile)
                put_tile(ref, level, width, z, row, pltpu.roll(tile_of(ref, level, 0, z, row), LANES - 1, 1))
                put_tile(ref, level, -1, z, row, pltpu.roll(tile_of(ref, level, width - 1, z, row), 1, 1))
    for strip in range(level.strips):
        shift = offsets[step, strip] // level.factor
        lane, page = shift // width, shift % width
        under = (strip - 1) % level.strips
        first = level.at(0, 0, SUB + strip * level.pitch)
        last = level.at(0, 0, SUB) + under * level.pitch + level.rows - 1
        upper = ref[pl.ds(first, count, stride=level.height), :]
        lower = ref[pl.ds(last, count, stride=level.height), :]
        start = strip * 4 * count
        halo[pl.ds(start, count), :] = pltpu.roll(upper, (LANES - lane) % LANES, 1)
        halo[pl.ds(start + count, count), :] = pltpu.roll(upper, LANES - 1 - lane, 1)
        halo[pl.ds(start + 2 * count, count), :] = pltpu.roll(lower, (lane + 1) % LANES, 1)
        halo[pl.ds(start + 3 * count, count), :] = pltpu.roll(lower, lane, 1)
        ref[pl.ds(last + 1, count, stride=level.height), :] = halo[pl.ds(start + page * level.planes, count), :]
        ref[pl.ds(first - 1, count, stride=level.height), :] = halo[
            pl.ds(start + 2 * count + (width - page) * level.planes, count), :
        ]


UNROLLED = 16


def repeat(count, body, carry):
    if count > UNROLLED:
        return lax.fori_loop(0, count, body, carry)
    for index in range(count):
        carry = body(index, carry)
    return carry


def stencil(ref, level, base):
    planes, width = level.planes, level.pages
    cell = [[tile_of(ref, level, p, z, base) for z in range(planes)] for p in range(-1, width + 1)]
    out = []
    for p in range(width):
        row = []
        for z in range(planes):
            left, here, right = cell[p][z], cell[p + 1][z], cell[p + 2][z]
            above = tile_of(ref, level, p, z, base + 1)
            below = tile_of(ref, level, p, z, base - 1)
            beside = (above + below) + (right + left)
            vertical = cell[p + 1][(z + 1) % planes] + cell[p + 1][(z - 1) % planes]
            row.append((here, right, left, beside, vertical))
        out.append(row)
    return out


def smooth(level, cell, beside, vertical):
    k = level.relax
    return (1.0 - k * level.diagonal) * cell + (k * level.coupling) * beside + (k * VERTICAL) * vertical


def apply(level, cell, beside, vertical):
    return level.diagonal * cell - level.coupling * beside - VERTICAL * vertical


def loop_coarse(coarse, body):
    count = coarse.strips * coarse.tiles
    if count <= 16:
        for index in range(count):
            body(index, 0)
    else:
        lax.fori_loop(0, count, body, 0)


def restrict(ref, level, coarse_ref, coarse, pairs):
    planes = level.planes

    def body(index, carry):
        strip, tile = index // coarse.tiles, index % coarse.tiles
        room = index * coarse.count * 2 * SUB if isinstance(index, int) else 0
        for half in range(2):
            base = level.base(strip, 2 * tile + half)
            terms = stencil(ref, level, base)
            for p in range(coarse.pages):
                for z in range(planes):
                    total = 0.0
                    for q in (2 * p, 2 * p + 1):
                        cell, _, _, beside, vertical = terms[q][z]
                        total = total + smooth(level, cell, beside, vertical)
                    pairs[pl.ds(room + (p * planes + z) * 2 * SUB + half * SUB, SUB), :] = total
        for p in range(coarse.pages):
            for z in range(planes):
                start = room + (p * planes + z) * 2 * SUB
                even = pairs[pl.ds(start, SUB, stride=2), :]
                odd = pairs[pl.ds(start + 1, SUB, stride=2), :]
                put_tile(coarse_ref, coarse, p, z, coarse.base(strip, tile), 0.25 * (even + odd))
        return carry

    loop_coarse(coarse, body)


def prolong(coarse_ref, coarse, residual, level, ref, pairs):
    planes = level.planes

    def body(index, carry):
        strip, tile = index // coarse.tiles, index % coarse.tiles
        room = index * coarse.count * 2 * SUB if isinstance(index, int) else 0
        for p in range(coarse.pages):
            for z in range(planes):
                start = room + (p * planes + z) * 2 * SUB
                value = tile_of(coarse_ref, coarse, p, z, coarse.base(strip, tile))
                pairs[pl.ds(start, SUB, stride=2), :] = value
                pairs[pl.ds(start + 1, SUB, stride=2), :] = value
        for p in range(coarse.pages):
            for z in range(planes):
                start = room + (p * planes + z) * 2 * SUB
                for half in range(2):
                    value = pairs[pl.ds(start + half * SUB, SUB), :]
                    base = level.base(strip, 2 * tile + half)
                    for q in (2 * p, 2 * p + 1):
                        put_tile(ref, level, q, z, base, level.relax * tile_of(residual, level, q, z, base) + value)
        return carry

    loop_coarse(coarse, body)


def per_tile(level, body, sums):
    def step(index, carry):
        return body(level.base(index // level.tiles, index % level.tiles), carry)

    zero = jnp.zeros((SUB, LANES), jnp.float32)
    return repeat(level.strips * level.tiles, step, (zero,) * sums)


def total(vector):
    return jnp.sum(jnp.sum(vector, axis=0, keepdims=True), axis=1, keepdims=True)


def relaxed(ref, residual, level, target):
    def body(base, carry):
        for p, row in enumerate(stencil(ref, level, base)):
            for z, (cell, _, _, beside, vertical) in enumerate(row):
                value = smooth(level, cell, beside, vertical) + level.relax * tile_of(residual, level, p, z, base)
                put_tile(target, level, p, z, base, value)
        return carry

    per_tile(level, body, 0)


def coarsest(residual, level, offsets, step, spare, halo):
    def first(base, carry):
        for p, row in enumerate(stencil(residual, level, base)):
            for z, (cell, _, _, beside, vertical) in enumerate(row):
                put_tile(spare[0], level, p, z, base, level.relax * (cell + smooth(level, cell, beside, vertical)))
        return carry

    fill_halo(residual, level, offsets, step, halo)
    per_tile(level, first, 0)
    now = 0
    for _ in range(COARSE - 2):
        fill_halo(spare[now], level, offsets, step, halo)
        relaxed(spare[now], residual, level, spare[1 - now])
        now = 1 - now
    return spare[now]


def vcycle(residual, levels, index, offsets, step, work, halo, pairs):
    level, coarse = levels[index], levels[index + 1]
    below, estimate = work[index + 1], work[index][1]
    fill_halo(residual, level, offsets, step, halo)
    restrict(residual, level, below[0], coarse, pairs)
    if index + 2 == LEVELS:
        correction = coarsest(below[0], coarse, offsets, step, below[1:], halo)
    else:
        vcycle(below[0], levels, index + 1, offsets, step, work, halo, pairs)
        correction = below[2]
        relaxed(below[1], below[0], coarse, correction)
    prolong(correction, coarse, residual, level, estimate, pairs)
    fill_halo(estimate, level, offsets, step, halo)


def swap_pages(pages, chosen):
    bit = 1
    while bit < len(pages):
        mask = chosen(bit)
        for p in range(len(pages)):
            if not p & bit:
                a, b = pages[p], pages[p | bit]
                pages[p], pages[p | bit] = jnp.where(mask, b, a), jnp.where(mask, a, b)
        bit *= 2
    return pages


def interleave(block, strips, level, gy, gx, targets, stage):
    width, planes = level.pages, level.planes
    lane = lax.broadcasted_iota(jnp.int32, (SUB, LANES), 1)
    per = LANES // width
    groups = [
        (name, dy, z, tile) for name in range(len(targets)) for dy in range(strips) for z in range(planes) for tile in range(level.tiles)
    ]
    sources = [lane % per * width + jnp.bitwise_xor(lane // per, jnp.bitwise_xor(gx, s)) for s in range(width)]
    for group, (name, dy, z, tile) in enumerate(groups):
        pages = [block(name, dy, p, z, tile) for p in range(width)]
        pages = swap_pages(pages, lambda bit: lane // bit % 2 == 1)
        for p in range(width):
            moved = jnp.take_along_axis(pages[p], sources[p], axis=1)
            stage[pl.ds((group * width + p) * SUB, SUB), :] = moved
    for group, (name, dy, z, tile) in enumerate(groups):
        row = level.base(jnp.bitwise_xor(gy, dy), tile)
        pages = [stage[pl.ds((group * width + p) * SUB, SUB), :] for p in range(width)]
        pages = swap_pages(pages, lambda bit: lane // (per * bit) % 2 == 1)
        for p in range(width):
            put_tile(targets[name], level, jnp.bitwise_xor(gx, p), z, row, pages[p])


def solve(offsets, u, v, r, q, w, work, halo, pairs, levels):
    fine = levels[0]
    e = work[0][1]
    update = None
    for step in range(STEPS):
        fill_halo(u, fine, offsets, step, halo)

        def residual(base, carry):
            for p, row in enumerate(stencil(u, fine, base)):
                for z, (cell, right, left, beside, vertical) in enumerate(row):
                    speed = tile_of(v, fine, p, z, base)
                    cube = cell * cell * cell
                    value = (
                        (1.0 + REACTION - fine.diagonal) * cell
                        - REACTION * cube
                        - ADVECTION * speed * (right - left)
                        + fine.coupling * beside
                        + VERTICAL * vertical
                    )
                    put_tile(r, fine, p, z, base, value)
            return carry

        per_tile(fine, residual, 0)
        vcycle(r, levels, 0, offsets, step, work, halo, pairs)

        def finish(base, carry):
            (rw,) = carry
            for p, row in enumerate(stencil(e, fine, base)):
                for z, (cell, _, _, beside, vertical) in enumerate(row):
                    res = tile_of(r, fine, p, z, base)
                    value = smooth(fine, cell, beside, vertical) + fine.relax * res
                    put_tile(w, fine, p, z, base, value)
                    rw = rw + res * value
            return (rw,)

        (rw,) = per_tile(fine, finish, 1)
        rw = total(rw)
        fill_halo(w, fine, offsets, step, halo)

        def image(base, carry):
            (wq,) = carry
            for p, row in enumerate(stencil(w, fine, base)):
                for z, (cell, _, _, beside, vertical) in enumerate(row):
                    value = apply(fine, cell, beside, vertical)
                    put_tile(q, fine, p, z, base, value)
                    wq = wq + cell * value
            return (wq,)

        (wq,) = per_tile(fine, image, 1)
        alpha = rw / total(wq)
        vcycle(q, levels, 0, offsets, step, work, halo, pairs)

        def finish_next(base, carry):
            (rw,) = carry
            for p, row in enumerate(stencil(e, fine, base)):
                for z, (cell, _, _, beside, vertical) in enumerate(row):
                    img = tile_of(q, fine, p, z, base)
                    value = smooth(fine, cell, beside, vertical) + fine.relax * img
                    res = tile_of(r, fine, p, z, base) - alpha * img
                    value = tile_of(w, fine, p, z, base) - alpha * value
                    put_tile(r, fine, p, z, base, value)
                    rw = rw + res * value
            return (rw,)

        (following,) = per_tile(fine, finish_next, 1)
        following = total(following)
        beta = following / rw
        fill_halo(r, fine, offsets, step, halo)

        def image_next(base, carry):
            (pq,) = carry
            for p, row in enumerate(stencil(r, fine, base)):
                for z, (cell, _, _, beside, vertical) in enumerate(row):
                    direction = cell + beta * tile_of(w, fine, p, z, base)
                    value = apply(fine, cell, beside, vertical) + beta * tile_of(q, fine, p, z, base)
                    pq = pq + direction * value
            return (pq,)

        (pq,) = per_tile(fine, image_next, 1)
        alpha_next = following / total(pq)
        along = alpha + alpha_next * beta

        def update(base, carry):
            for p in range(fine.pages):
                for z in range(fine.planes):
                    value = (
                        tile_of(u, fine, p, z, base)
                        + along * tile_of(w, fine, p, z, base)
                        + alpha_next * tile_of(r, fine, p, z, base)
                    )
                    put_tile(u, fine, p, z, base, value)
            return carry

        if step + 1 < STEPS:
            per_tile(fine, update, 0)
    return update


def whole_kernel(places, arrays, levels, *refs):
    offsets, held, out = refs[0], refs[1 : 1 + arrays], refs[1 + arrays]
    u, v, r, q, w, e, r1, e1, f1, r2, e2, f2, halo, pairs, stage = refs[2 + arrays :]
    fine = levels[0]
    gy, gx = lax.axis_index("gy"), lax.axis_index("gx")

    def block(name, dy, dx, z, tile):
        array, place = places[name, dy, dx]
        return held[array][(*place, z, pl.ds(tile * SUB, SUB), slice(None))]

    interleave(block, fine.strips, fine, gy, gx, (u, v), stage)
    work = [[r, e], [r1, e1, f1], [r2, e2, f2]]
    update = solve(offsets, u, v, r, q, w, work, halo, pairs, levels)
    lane = lax.broadcasted_iota(jnp.int32, (SUB, LANES), 1)
    source = gx * (LANES // fine.pages) + lane // fine.pages
    for tile in range(fine.tiles):
        base = fine.base(gy, tile)
        update(base, ())
        for z in range(fine.planes):
            value = jnp.zeros((SUB, LANES), jnp.float32)
            for p in range(fine.pages):
                page = jnp.take_along_axis(tile_of(u, fine, p, z, base), source, axis=1)
                value = jnp.where(lane % fine.pages == p, page, value)
            out[z, pl.ds(tile * SUB, SUB), :] = value


def on_whole(arrays, places, offsets, strips, width):
    planes, rows, columns = arrays[0].shape[-3:]
    levels = [Level(i, width, rows, strips, planes) for i in range(LEVELS)]
    fields = [pltpu.VMEM(levels[0].shape(), jnp.float32)] * 6
    fields += [pltpu.VMEM(levels[1].shape(), jnp.float32)] * 3 + [pltpu.VMEM(levels[2].shape(), jnp.float32)] * 3
    count = levels[0].count
    scratch = fields + [
        pltpu.VMEM((strips * 4 * count, LANES), jnp.float32),
        pltpu.VMEM((planes * strips * rows * width // 2, LANES), jnp.float32),
        pltpu.VMEM((2 * planes * strips * rows * width, LANES), jnp.float32),
    ]

    def kernel(*refs):
        whole_kernel(places, len(arrays), levels, *refs)

    return pl.pallas_call(
        kernel,
        out_shape=jax.ShapeDtypeStruct((planes, rows, columns), jnp.float32),
        in_specs=[pl.BlockSpec(memory_space=pltpu.SMEM)] + [pl.BlockSpec(memory_space=pltpu.VMEM)] * len(arrays),
        out_specs=pl.BlockSpec(memory_space=pltpu.VMEM),
        scratch_shapes=scratch,
        compiler_params=pltpu.CompilerParams(vmem_limit_bytes=48 << 20),
    )(offsets, *arrays)


def swapped(block, axis, bits):
    count = lax.axis_size(axis)
    return lax.ppermute(block, axis, [(i, i ^ bits) for i in range(count)])


def gathered(phase, velocity):
    width = lax.axis_size("gx")
    steps = list(range(0, width, 2))
    both = jnp.stack([phase, velocity])
    cut = len(steps) // 2
    far = [swapped(both, "gx", k) for k in steps[cut:]]
    arrays, places = [], {}
    for name, own in enumerate((phase, velocity)):
        got = [swapped(own[None], "gx", k) for k in steps[1:cut]]
        line = jnp.concatenate([both[name : name + 1]] + got + [block[name : name + 1] for block in far])
        across = swapped(line, "gx", 1)
        along = swapped(line, "gy", 2)
        corner = swapped(along, "gx", 1) if name else swapped(across, "gy", 2)
        for dy, dx, array in ((0, 0, line), (0, 1, across), (2, 0, along), (2, 1, corner)):
            for core in range(2):
                for i, k in enumerate(steps):
                    places[name, dy ^ core, dx ^ k] = (len(arrays), (i,))
                arrays.append(swapped(array, "gy", 1) if core else array)
    return arrays, places


def padded(cells, sides, width):
    for axis, dim in sides:
        count = lax.axis_size(axis)
        head = lax.slice_in_dim(cells, 0, width, axis=dim)
        tail = lax.slice_in_dim(cells, cells.shape[dim] - width, cells.shape[dim], axis=dim)
        cells = jnp.concatenate(
            [
                lax.ppermute(tail, axis, [(i, (i + 1) % count) for i in range(count)]),
                cells,
                lax.ppermute(head, axis, [((i + 1) % count, i) for i in range(count)]),
            ],
            axis=dim,
        )
    return cells


def sheared(bottom_row, upper_row, offsets_now, anchor, columns):
    breadth = bottom_row.shape[1]
    device_row = lax.axis_index("gy")
    row_count = lax.axis_size("gy")
    below_shift = offsets_now[device_row]
    above_shift = offsets_now[(device_row + 1) % row_count]
    local_columns = jnp.arange(columns, dtype=jnp.int32)
    down_index = (anchor + below_shift + local_columns) % breadth
    up_index = (anchor - above_shift + local_columns) % breadth
    down_window = jnp.take(bottom_row, down_index, axis=1)
    up_window = jnp.take(upper_row, up_index, axis=1)
    stacked = jnp.stack([down_window, up_window], axis=1)
    rims = padded(stacked, (("gy", 1),), 1)
    return (rims[:, 0, :], rims[:, 3, :])


def block_stencil(field, below_row, above_row, across, coupling):
    diagonal = 1.0 + 4.0 * coupling + 2.0 * VERTICAL
    column_pad = jnp.concatenate([below_row[:, None, :], field, above_row[:, None, :]], axis=1)
    beside = column_pad[:, 2:, :] + column_pad[:, :-2, :] + across
    vertical_sum = jnp.roll(field, 1, 0) + jnp.roll(field, -1, 0)
    return diagonal * field - coupling * beside - VERTICAL * vertical_sum


def block_operate(field, offsets_now, coupling):
    columns = field.shape[2]
    margins = padded(field, (("gx", 2),), 1)
    bottom_full, upper_full = (
        lax.all_gather(field[:, 0, :], "gx", axis=1, tiled=True),
        lax.all_gather(field[:, -1, :], "gx", axis=1, tiled=True),
    )
    right_field = margins[:, :, 2:]
    left_field = margins[:, :, :-2]
    below_row, above_row = sheared(
        bottom_full, upper_full, offsets_now, lax.axis_index("gx") * columns, columns
    )
    across = right_field + left_field
    return (block_stencil(field, below_row, above_row, across, coupling), right_field, left_field)


def block_operate_strip(field, offsets_now, coupling):
    below_row, above_row = sheared(field[:, 0, :], field[:, -1, :], offsets_now, 0, field.shape[2])
    across = jnp.roll(field, 1, 2) + jnp.roll(field, -1, 2)
    return block_stencil(field, below_row, above_row, across, coupling)


def block_coarsest(residual, offsets_now, coupling):
    diagonal = 1.0 + 4.0 * coupling + 2.0 * VERTICAL
    columns = residual.shape[2]
    gathered = lax.all_gather(residual, "gx", axis=2, tiled=True)
    estimate = RELAXATION * gathered / diagonal
    for sweep_index in range(COARSE - 1):
        estimate = (
            estimate
            + RELAXATION * (gathered - block_operate_strip(estimate, offsets_now, coupling)) / diagonal
        )
    return lax.dynamic_slice_in_dim(estimate, lax.axis_index("gx") * columns, columns, 2)


def block_vcycle(residual, offsets_raw, layer_index):
    factor = 2**layer_index
    coupling = DIFFUSION / 4.0**layer_index
    diagonal = 1.0 + 4.0 * coupling + 2.0 * VERTICAL
    offsets_now = offsets_raw // factor
    if layer_index == LEVELS - 1:
        return block_coarsest(residual, offsets_now, coupling)
    estimate = RELAXATION * residual / diagonal
    defect = residual - block_operate(estimate, offsets_now, coupling)[0]
    planes, height, breadth = defect.shape
    coarser = defect.reshape(planes, height // 2, 2, breadth // 2, 2).mean(axis=(2, 4))
    correction = block_vcycle(coarser, offsets_raw, layer_index + 1)
    estimate = estimate + jnp.repeat(jnp.repeat(correction, 2, axis=1), 2, axis=2)
    estimate = (
        estimate + RELAXATION * (residual - block_operate(estimate, offsets_now, coupling)[0]) / diagonal
    )
    return estimate


def total_inner(first_field, second_field):
    return lax.psum(jnp.sum(first_field * second_field), ("gy", "gx"))


def spread(phase, velocity, offsets):
    phase_now = phase
    for time_step in range(STEPS):
        offsets_raw = offsets[time_step]
        applied, right_field, left_field = block_operate(phase_now, offsets_raw, DIFFUSION)
        source = (
            phase_now
            + REACTION * (phase_now - phase_now * phase_now * phase_now)
            - ADVECTION * velocity * (right_field - left_field)
        )
        residual = source - applied
        precond = block_vcycle(residual, offsets_raw, 0)
        projected = total_inner(residual, precond)
        direction = precond
        for iteration in range(ITERS):
            image = block_operate(direction, offsets_raw, DIFFUSION)[0]
            step_size = projected / total_inner(direction, image)
            phase_now = phase_now + step_size * direction
            residual = residual - step_size * image
            if iteration + 1 < ITERS:
                precond = block_vcycle(residual, offsets_raw, 0)
                following = total_inner(residual, precond)
                direction = precond + following / projected * direction
                projected = following
    return phase_now


MOST_DEVICES = 32
MOST_BYTES = 44 << 20


def local(phase, velocity, offsets):
    strips, width = lax.axis_size("gy"), lax.axis_size("gx")
    planes, rows, columns = phase.shape
    sizes = Level(0, width, rows, strips, planes).shape()
    fits = 10 * 4 * sizes[0] * sizes[1] < MOST_BYTES and strips * width <= MOST_DEVICES
    shaped = columns == LANES and rows % 32 == 0 and width in (8, 16, 32, 64) and strips == 4
    if fits and shaped:
        return on_whole(*gathered(phase, velocity), offsets, strips, width)
    return spread(phase, velocity, offsets)


def solution(mesh):
    placed = (P(None, "gy", "gx"), P(None, "gy", "gx"), P())
    return jax.shard_map(local, mesh=mesh, in_specs=placed, out_specs=P(None, "gy", "gx"), check_vma=False)
```
